32 devices in a mesh: dp: 4 (over z), blk: 2 (over core), head: 4 (over y, x).
Axes of the slice: x: 2, y: 2, z: 4, core: 2. Of those that a mesh axis runs over, the one named last changes fastest.
Arguments:
- stream_in: float32 [8, 2048, 1024], P('dp', ('blk', 'head')), may hold values from -6 to 6
- ln1_gain: bfloat16 [1024], P(('dp', 'blk', 'head')), may hold values from 0.5 to 1.5
- ln1_bias: bfloat16 [1024], P(('dp', 'blk', 'head')), may hold values from -1 to 1
- w_qkv: bfloat16 [1024, 3072], P(('dp', 'blk', 'head')), may hold values from -1 to 1, as said below
- b_qv: bfloat16 [2, 1024], P(None, ('dp', 'blk', 'head')), may hold values from -1 to 1
- w_out: bfloat16 [1024, 1024], P(('dp', 'blk', 'head')), may hold values from -1 to 1
- b_out: bfloat16 [1024], P(('dp', 'blk', 'head')), may hold values from -1 to 1
- ln2_gain: bfloat16 [1024], P(('dp', 'blk', 'head')), may hold values from 0.5 to 1.5
- ln2_bias: bfloat16 [1024], P(('dp', 'blk', 'head')), may hold values from -1 to 1
- w_fc: bfloat16 [1024, 4096], P(('dp', 'blk', 'head')), may hold values from -0.1875 to 0.1875
- b_fc: bfloat16 [4096], P(('dp', 'blk', 'head')), may hold values from -1 to 1
- w_proj: bfloat16 [4096, 1024], P(('dp', 'blk', 'head')), may hold values from -0.09375 to 0.09375
- b_proj: bfloat16 [1024], P(('dp', 'blk', 'head')), may hold values from -1 to 1
- cotangent: float32 [8, 2048, 1024], P('dp', ('blk', 'head')), may hold values from -6 to 6
Outputs:
- stream_out: float32 [8, 2048, 1024], P('dp', ('blk', 'head'))
- grad_in: float32 [8, 2048, 1024], P('dp', ('blk', 'head'))
- grad_ln1_gain: float32 [1024], P(('dp', 'blk', 'head'))
- grad_ln1_bias: float32 [1024], P(('dp', 'blk', 'head'))
- grad_w_qkv: float32 [1024, 3072], P(('dp', 'blk', 'head'))
- grad_b_qv: float32 [2, 1024], P(None, ('dp', 'blk', 'head'))
- grad_w_out: float32 [1024, 1024], P(('dp', 'blk', 'head'))
- grad_b_out: float32 [1024], P(('dp', 'blk', 'head'))
- grad_ln2_gain: float32 [1024], P(('dp', 'blk', 'head'))
- grad_ln2_bias: float32 [1024], P(('dp', 'blk', 'head'))
- grad_w_fc: float32 [1024, 4096], P(('dp', 'blk', 'head'))
- grad_b_fc: float32 [4096], P(('dp', 'blk', 'head'))
- grad_w_proj: float32 [4096, 1024], P(('dp', 'blk', 'head'))
- grad_b_proj: float32 [1024], P(('dp', 'blk', 'head'))
The draws below stay inside these ranges and needn't reach their ends.
Inputs may be any that keep to these rules, and one draw needn't show every extreme that they name: `w_qkv`: entries are real numbers of order 1024 ** -0.5.
All inputs are finite; a program needn't handle non-finite values.
Results may differ from the reference program's by a relative error of at most 0.0095.
Values may be sent and summed in bfloat16 or wider, within the bound.
No kernel may reach another device: no remote copies, remote signals or barrier semaphores. Data moves between devices by JAX's collectives and lax.ppermute only.
A program may use at most 256 MiB of HBM per device.

```python
import math
import jax
import jax.numpy as jnp
from jax import lax

D = 1024
H = 16
HD = 64
FF = 4096
L = 2048
SEQS = 8


def draw_w_qkv(key, part):
    first_key = jax.random.fold_in(key, 17)
    base = jax.random.truncated_normal(first_key, -6.0, 6.0, (D, 3 * D), jnp.float32)
    return (base * D ** (-0.5)).astype(jnp.bfloat16)


def with_spikes(values, key, source, target, parts, factor):
    owner, partner = [(jnp.arange(values.shape[dim]) // (values.shape[dim] // parts)).reshape([-1 if axis == dim else 1 for axis in range(values.ndim)]) for dim in (source, target)]
    chosen = jax.random.permutation(key, parts)[partner]
    strong = (owner == chosen) | (owner == (partner + parts // 2) % parts)
    return jnp.where(strong, factor * values, values)


def block_levels(key, extent, cuts, least, largest):
    def one(position, blocks):
        steps = jax.random.uniform(jax.random.fold_in(jax.random.fold_in(key, 6), position), (blocks,), jnp.float32, least / len(cuts), largest / len(cuts))
        return jnp.repeat(jnp.exp(steps), extent[position] // blocks).reshape((-1,) + (1,) * (len(extent) - position - 1))

    loudness = one(*cuts[0])
    for cut in cuts[1:]:
        loudness = loudness * one(*cut)
    return loudness


def noise(own_key, extent, scale, bound, shards=(), kind=jnp.bfloat16):
    loudness = block_levels(own_key, extent, shards, -0.22, 0.18) if shards else 1.0
    values = jax.random.normal(own_key, extent, jnp.float32) * scale * loudness
    return jnp.minimum(jnp.maximum(values, -bound), bound).astype(kind)


def noise_with(rng, dims, scale, most, shards, heavy, dtype=jnp.bfloat16):
    entries = scale * jax.random.normal(rng, dims, jnp.float32)
    if shards:
        entries = entries * block_levels(rng, dims, shards, -0.22, 0.18)
    return jnp.clip(with_spikes(entries, jax.random.fold_in(rng, 3), *heavy), -most, most).astype(dtype)


def setup_inputs(seed: int = 0) -> dict:
    seeds = jax.random.split(jax.random.key(seed), 15)
    stream_in = noise(seeds[0], (SEQS, L, D), 1.0, 6.0, ((0, 4), (1, 8)), jnp.float32)
    ln1_gain = jnp.clip(1.0 + 0.1 * jax.random.normal(seeds[1], (D,), jnp.float32), 0.5, 1.5).astype(jnp.bfloat16)
    ln1_bias = noise(seeds[2], (D,), 0.2, 1.0, ((0, 32),))
    w_qkv = draw_w_qkv(jax.random.fold_in(seeds[14], 71), 0)
    b_qv = noise(seeds[4], (2, D), 0.2, 1.0, ((1, 32),))
    w_out = noise(seeds[5], (D, D), (D // 32) ** -0.5, 1.0, ((0, 32),))
    b_out = noise(seeds[6], (D,), 0.2, 1.0, ((0, 32),))
    ln2_gain = jnp.clip(1.0 + 0.1 * jax.random.normal(seeds[7], (D,), jnp.float32), 0.5, 1.5).astype(jnp.bfloat16)
    ln2_bias = noise(seeds[8], (D,), 0.2, 1.0, ((0, 32),))
    w_fc = noise(seeds[9], (D, FF), D ** -0.5, 0.1875, ((0, 32),))
    b_fc = noise(seeds[10], (FF,), 0.2, 1.0, ((0, 32),))
    w_proj = noise(seeds[11], (FF, D), FF ** -0.5, 0.09375, ((0, 32),))
    b_proj = noise(seeds[12], (D,), 0.2, 1.0, ((0, 32),))
    cotangent = noise_with(seeds[13], (SEQS, L, D), 1.0, 6.0, ((0, 4), (1, 8)), (1, 2, 8, 2.0), jnp.float32)
    return dict(stream_in=stream_in, ln1_gain=ln1_gain, ln1_bias=ln1_bias, w_qkv=w_qkv, b_qv=b_qv, w_out=w_out, b_out=b_out, ln2_gain=ln2_gain, ln2_bias=ln2_bias, w_fc=w_fc, b_fc=b_fc, w_proj=w_proj, b_proj=b_proj, cotangent=cotangent)


EPSILON = 1e-05
GELU_COEF = 0.044715
ROOT_TWO_PI = math.sqrt(2.0 / math.pi)

def normalize(stream):
    centred = stream - lax.optimization_barrier(jnp.mean(stream, axis=-1, keepdims=True))
    inv_std = lax.rsqrt(lax.optimization_barrier(jnp.mean(centred * centred, axis=-1, keepdims=True)) + EPSILON)
    return (centred * inv_std, inv_std)

def norm_back(grad_normed, normed, inv_std):
    return inv_std * (grad_normed - lax.optimization_barrier(jnp.mean(grad_normed, axis=-1, keepdims=True)) - normed * lax.optimization_barrier(jnp.mean(grad_normed * normed, axis=-1, keepdims=True)))

def gelu_pair(pre_act):
    tangent = jnp.tanh(ROOT_TWO_PI * (pre_act + GELU_COEF * pre_act * pre_act * pre_act))
    value = 0.5 * pre_act * (1.0 + tangent)
    slope = 0.5 * (1.0 + tangent) + 0.5 * pre_act * (1.0 - tangent * tangent) * ROOT_TWO_PI * (1.0 + 3.0 * GELU_COEF * pre_act * pre_act)
    return (value, slope)

def matmul(left, right):
    return jnp.dot(left, right, preferred_element_type=jnp.float32)

def matmul_tn(left, right):
    return lax.dot_general(left, right, (((0,), (0,)), ((), ())), preferred_element_type=jnp.float32)

def matmul_nt(left, right):
    return lax.dot_general(left, right, (((1,), (1,)), ((), ())), preferred_element_type=jnp.float32)

def masked_scores(queries, keys, start, qblock):
    count = start + qblock
    scale = 1.0 / math.sqrt(HD)
    scores = jnp.einsum('qhd,khd->hqk', queries[start:count].astype(jnp.float32), keys[:count].astype(jnp.float32)) * scale
    row_pos = start + jnp.arange(qblock)[:, None]
    column = jnp.arange(count)[None, :]
    return (jnp.where((column <= row_pos)[None], scores, -jnp.inf), count)

def attend(queries, keys, values):
    qblock = min(512, L)
    outputs = []
    lse_list = []
    for start in range(0, L, qblock):
        scores, count = masked_scores(queries, keys, start, qblock)
        top = lax.optimization_barrier(jnp.max(scores, axis=-1, keepdims=True))
        lse = top + jnp.log(lax.optimization_barrier(jnp.sum(jnp.exp(scores - top), axis=-1, keepdims=True)))
        probs_low = jnp.exp(scores - lse).astype(jnp.bfloat16)
        result = jnp.einsum('hqk,khd->qhd', probs_low.astype(jnp.float32), values[:count].astype(jnp.float32))
        outputs.append(result.astype(jnp.bfloat16))
        lse_list.append(lse)
    return (jnp.concatenate(outputs, axis=0), lse_list)

def attend_back(queries, keys, values, attn, grad_attn, lse_list):
    qblock = min(512, L)
    scale = 1.0 / math.sqrt(HD)
    grad_keys = jnp.zeros((L, H, HD), jnp.float32)
    grad_values = jnp.zeros((L, H, HD), jnp.float32)
    grad_queries = []
    for block_index, start in enumerate(range(0, L, qblock)):
        scores, count = masked_scores(queries, keys, start, qblock)
        probs = jnp.exp(scores - lse_list[block_index])
        probs_low = probs.astype(jnp.bfloat16).astype(jnp.float32)
        grad_rows = grad_attn[start:count].astype(jnp.float32)
        delta = lax.optimization_barrier(jnp.sum(grad_rows * attn[start:count].astype(jnp.float32), axis=-1))
        delta = jnp.transpose(delta, (1, 0))[:, :, None]
        dprob = jnp.einsum('qhd,khd->hqk', grad_rows, values[:count].astype(jnp.float32))
        dscore = (probs * (dprob - delta) * scale).astype(jnp.bfloat16).astype(jnp.float32)
        grad_queries.append(jnp.einsum('hqk,khd->qhd', dscore, keys[:count].astype(jnp.float32)))
        query_rows = queries[start:count].astype(jnp.float32)
        grad_keys = grad_keys.at[:count].add(jnp.einsum('hqk,qhd->khd', dscore, query_rows))
        grad_values = grad_values.at[:count].add(jnp.einsum('hqk,qhd->khd', probs_low, grad_rows))
    grad_q = jnp.concatenate(grad_queries, axis=0).astype(jnp.bfloat16)
    return (grad_q, grad_keys.astype(jnp.bfloat16), grad_values.astype(jnp.bfloat16))

def one_sequence(seq_in, seq_cot, params):
    ln1_gain, ln1_bias, w_qkv, b_qv, w_out, b_out, ln2_gain, ln2_bias, w_fc, b_fc, w_proj, b_proj = params
    gain_one = ln1_gain.astype(jnp.float32)
    gain_two = ln2_gain.astype(jnp.float32)
    normed_one, inv_one = normalize(seq_in)
    act_one = (normed_one * gain_one + ln1_bias.astype(jnp.float32)).astype(jnp.bfloat16)
    qkv_bias = jnp.concatenate([b_qv[0].astype(jnp.float32), jnp.zeros((D,), jnp.float32), b_qv[1].astype(jnp.float32)])
    qkv = (matmul(act_one, w_qkv) + qkv_bias).astype(jnp.bfloat16)
    queries = qkv[:, :D].reshape(L, H, HD)
    keys = qkv[:, D:2 * D].reshape(L, H, HD)
    values = qkv[:, 2 * D:].reshape(L, H, HD)
    attn, lse_list = attend(queries, keys, values)
    attn_flat = attn.reshape(L, D)
    resid = seq_in + matmul(attn_flat, w_out) + b_out.astype(jnp.float32)
    normed_two, inv_two = normalize(resid)
    ctx = (normed_two * gain_two + ln2_bias.astype(jnp.float32)).astype(jnp.bfloat16)
    pre_act = matmul(ctx, w_fc) + b_fc.astype(jnp.float32)
    gelu_val, gelu_slope = gelu_pair(pre_act)
    hidden = gelu_val.astype(jnp.bfloat16)
    seq_out = resid + matmul(hidden, w_proj) + b_proj.astype(jnp.float32)
    cot_low = seq_cot.astype(jnp.bfloat16)
    grad_b_proj = lax.optimization_barrier(jnp.sum(seq_cot, axis=0))
    grad_w_proj = matmul_tn(hidden, cot_low)
    grad_pre = matmul_nt(cot_low, w_proj) * gelu_slope
    grad_b_fc = lax.optimization_barrier(jnp.sum(grad_pre, axis=0))
    pre_low = grad_pre.astype(jnp.bfloat16)
    grad_w_fc = matmul_tn(ctx, pre_low)
    grad_ctx = matmul_nt(pre_low, w_fc)
    grad_ln2_gain = lax.optimization_barrier(jnp.sum(grad_ctx * normed_two, axis=0))
    grad_ln2_bias = lax.optimization_barrier(jnp.sum(grad_ctx, axis=0))
    grad_resid = seq_cot + norm_back(grad_ctx * gain_two, normed_two, inv_two)
    grad_b_out = lax.optimization_barrier(jnp.sum(grad_resid, axis=0))
    resid_low = grad_resid.astype(jnp.bfloat16)
    grad_w_out = matmul_tn(attn_flat, resid_low)
    grad_attn = matmul_nt(resid_low, w_out).astype(jnp.bfloat16).reshape(L, H, HD)
    grad_q, grad_k, grad_v = attend_back(queries, keys, values, attn, grad_attn, lse_list)
    grad_qkv = jnp.concatenate([grad_q.reshape(L, D), grad_k.reshape(L, D), grad_v.reshape(L, D)], axis=1)
    grad_b_qv = jnp.stack([lax.optimization_barrier(jnp.sum(grad_q.reshape(L, D).astype(jnp.float32), axis=0)), lax.optimization_barrier(jnp.sum(grad_v.reshape(L, D).astype(jnp.float32), axis=0))])
    grad_w_qkv = matmul_tn(act_one, grad_qkv)
    grad_act = matmul_nt(grad_qkv, w_qkv)
    grad_ln1_gain = lax.optimization_barrier(jnp.sum(grad_act * normed_one, axis=0))
    grad_ln1_bias = lax.optimization_barrier(jnp.sum(grad_act, axis=0))
    grad_seq = grad_resid + norm_back(grad_act * gain_one, normed_one, inv_one)
    terms = (grad_ln1_gain, grad_ln1_bias, grad_w_qkv, grad_b_qv, grad_w_out, grad_b_out, grad_ln2_gain, grad_ln2_bias, grad_w_fc, grad_b_fc, grad_w_proj, grad_b_proj)
    return (seq_out, grad_seq, terms)

def reference(stream_in, ln1_gain, ln1_bias, w_qkv, b_qv, w_out, b_out, ln2_gain, ln2_bias, w_fc, b_fc, w_proj, b_proj, cotangent):
    params = (ln1_gain, ln1_bias, w_qkv, b_qv, w_out, b_out, ln2_gain, ln2_bias, w_fc, b_fc, w_proj, b_proj)

    def per_sequence(totals, pair_in):
        seq_out, grad_seq, terms = one_sequence(pair_in[0], pair_in[1], params)
        totals = tuple((total + term for total, term in zip(totals, terms)))
        return (totals, (seq_out, grad_seq))
    start_totals = tuple((jnp.zeros(weight.shape, jnp.float32) for weight in params))
    totals, outputs = lax.scan(per_sequence, start_totals, (stream_in, cotangent))
    return (outputs[0], outputs[1], totals[0], totals[1], totals[2], totals[3], totals[4], totals[5], totals[6], totals[7], totals[8], totals[9], totals[10], totals[11])
```

```python
import functools
import math

import jax
import jax.numpy as jnp
from jax import lax
from jax.experimental import pallas as pl
from jax.experimental.pallas import tpu as pltpu
from jax.sharding import PartitionSpec as P

HD = 64
EPSILON = 1e-05
GELU_COEF = 0.044715
ROOT_TWO_PI = math.sqrt(2.0 / math.pi)
SCALE = 1.0 / math.sqrt(HD)
LOG2E = math.log2(math.e)
F32 = jnp.float32
BF16 = jnp.bfloat16
VMEM_LIMIT = 48 * 1024 * 1024


def normalize(stream):
    centred = stream - jnp.mean(stream, axis=-1, keepdims=True)
    inv_std = lax.rsqrt(jnp.mean(centred * centred, axis=-1, keepdims=True) + EPSILON)
    return (centred * inv_std, inv_std)


def norm_back(grad_normed, normed, inv_std):
    return inv_std * (
        grad_normed
        - jnp.mean(grad_normed, axis=-1, keepdims=True)
        - normed * jnp.mean(grad_normed * normed, axis=-1, keepdims=True)
    )


def gelu_pair(pre_act):
    tangent = jnp.tanh(ROOT_TWO_PI * (pre_act + GELU_COEF * pre_act * pre_act * pre_act))
    value = 0.5 * pre_act * (1.0 + tangent)
    slope = 0.5 * (1.0 + tangent) + 0.5 * pre_act * (1.0 - tangent * tangent) * ROOT_TWO_PI * (
        1.0 + 3.0 * GELU_COEF * pre_act * pre_act
    )
    return (value, slope)


def dot(left, right, left_dim, right_dim):
    return lax.dot_general(
        left, right, (((left_dim,), (right_dim,)), ((), ())), preferred_element_type=F32
    )


def to_xor(value, step):
    count = lax.axis_size("head")
    return lax.ppermute(value, "head", [(i, i ^ step) for i in range(count)])


def to_shift(value, step):
    count = lax.axis_size("dp")
    return lax.ppermute(value, "dp", [(i, (i + step) % count) for i in range(count)])


def to_other_core(value):
    return lax.ppermute(value, "blk", [(0, 1), (1, 0)])


def pick(stacked, index, axis=0):
    return lax.dynamic_index_in_dim(stacked, index, axis, keepdims=False)


def by_half(core, own, other):
    return jnp.where(core == 0, jnp.stack([own, other]), jnp.stack([other, own]))


def place_kernel(counts, ids, *refs):
    dp_count, _, head_count = counts
    pieces, out, sem = refs[: 2 * head_count], refs[2 * head_count], refs[2 * head_count + 1]
    dp, core, head = ids[0], ids[1], ids[2]
    copies = []
    for which in range(2):
        for slot in range(head_count):
            for step in range(dp_count):
                source = lax.rem(dp + (dp_count - step), dp_count)
                copies.append(
                    pltpu.make_async_copy(
                        pieces[which * head_count + slot].at[step],
                        out.at[source, core ^ which, head ^ slot],
                        sem.at[len(copies)],
                    )
                )
    for copy in copies:
        copy.start()
    for copy in copies:
        copy.wait()


def place(pieces, ids):
    counts = (lax.axis_size("dp"), 2, lax.axis_size("head"))
    shape = pieces[0].shape[1:]
    return pl.pallas_call(
        functools.partial(place_kernel, counts),
        out_shape=jax.ShapeDtypeStruct(counts + shape, pieces[0].dtype),
        grid_spec=pltpu.PrefetchScalarGridSpec(
            num_scalar_prefetch=1,
            grid=(1,),
            in_specs=[pl.BlockSpec(memory_space=pl.ANY)] * len(pieces),
            out_specs=pl.BlockSpec(memory_space=pl.ANY),
            scratch_shapes=[pltpu.SemaphoreType.DMA((counts[0] * 2 * counts[2],))],
        ),
        name="place",
    )(ids, *pieces)


def gather_z(shard):
    return jnp.stack([shard] + [to_shift(shard, k) for k in range(1, lax.axis_size("dp"))])


def gather_plane(own):
    return [own] + [to_xor(own, j) for j in range(1, lax.axis_size("head"))]


def gather_rows(shard, ids):
    mine = gather_plane(gather_z(shard))
    theirs = [to_other_core(piece) for piece in mine]
    return place(mine + theirs, ids)


def scatter_rows(grad, core, head, dp):
    dp_count, _, head_count = grad.shape[:3]
    plane = []
    for slot in range(head_count):
        row = pick(grad, head ^ slot, 2)
        arrived = to_other_core(pick(row, 1 - core, 1))
        both = pick(row, core, 1).astype(F32) + arrived.astype(F32)
        plane.append(both if slot == 0 else to_xor(both.astype(BF16), slot))
    total = plane[0]
    for piece in plane[1:]:
        total = total + piece.astype(F32)
    low = total.astype(BF16)
    result = pick(total, dp)
    for step in range(1, dp_count):
        result = result + to_shift(pick(low, lax.rem(dp + step, dp_count)), step).astype(F32)
    return result


def gather_small(vector, ids):
    dp_count, head_count = lax.axis_size("dp"), lax.axis_size("head")
    rows = gather_z(vector[None])
    rows = jnp.stack(gather_plane(rows))
    rows = jnp.stack([rows, to_other_core(rows)])
    total = 2 * head_count * dp_count
    slot = jnp.arange(total)
    which, plane, step = slot // (head_count * dp_count), (slot // dp_count) % head_count, slot % dp_count
    source = ((ids[0] - step) % dp_count) * 2 * head_count + (ids[1] ^ which) * head_count + (ids[2] ^ plane)
    chosen = (source[None, :] == jnp.arange(total)[:, None]).astype(F32)
    return jnp.dot(chosen, rows.reshape(total, -1), precision=lax.Precision.HIGHEST)


def scatter_small(rows, core, head, dp):
    dp_count, _, head_count = rows.shape[:3]
    half = pick(rows, core, 1) + to_other_core(pick(rows, 1 - core, 1))
    total = pick(half, head, 1)
    for slot in range(1, head_count):
        total = total + to_xor(pick(half, head ^ slot, 1), slot)
    result = pick(total, dp)
    for step in range(1, dp_count):
        result = result + to_shift(pick(total, lax.rem(dp + step, dp_count)), step)
    return result


SLOTS = 4


def causal(block):
    key = lax.broadcasted_iota(jnp.int32, (block, block), 0)
    query = lax.broadcasted_iota(jnp.int32, (block, block), 1)
    return key <= query


def forward_kernel(block, me_ref, qkv, out, lse, scores_a, scores_b):
    me = me_ref[0]
    factor = SCALE * LOG2E
    mask = causal(block)

    def part(which, pos):
        return qkv[(pos % SLOTS) ^ me, which, :, pl.ds((pos // SLOTS) * block, block)]

    for row in range(2 * SLOTS):
        scores = scores_a if row % 2 == 0 else scores_b
        query = part(0, row)
        top = None
        for col in range(row + 1):
            tile = dot(part(1, col), query, 0, 0)
            if col == row:
                tile = jnp.where(mask, tile, -jnp.inf)
            scores[pl.ds(col * block, block), :] = tile
            high = jnp.max(tile, axis=0, keepdims=True)
            top = high if top is None else jnp.maximum(top, high)
        shift = top * factor
        total = jnp.zeros_like(top)
        result = jnp.zeros((HD, block), F32)
        for col in range(row + 1):
            probs = jnp.exp2(scores[pl.ds(col * block, block), :] * factor - shift)
            total = total + jnp.sum(probs, axis=0, keepdims=True)
            result = result + dot(part(2, col), probs.astype(BF16), 1, 0)
        out[(row % SLOTS) ^ me, :, pl.ds((row // SLOTS) * block, block)] = (result / total).astype(BF16)
        lse[pl.ds(row, 1), :] = shift + jnp.log2(total)


def backward_kernel(block, me_ref, qkv, attn, grad_attn, lse, out, grad_q, delta):
    me = me_ref[0]
    factor = SCALE * LOG2E
    mask = causal(block)

    def part(which, pos):
        return qkv[(pos % SLOTS) ^ me, which, :, pl.ds((pos // SLOTS) * block, block)]

    def tokens(ref, pos):
        return ref[(pos % SLOTS) ^ me, :, pl.ds((pos // SLOTS) * block, block)]

    for row in range(2 * SLOTS):
        product = tokens(grad_attn, row).astype(F32) * tokens(attn, row).astype(F32)
        delta[pl.ds(row, 1), :] = jnp.sum(product, axis=0, keepdims=True)
    for col in range(2 * SLOTS):
        key, value = part(1, col), part(2, col)
        grad_key = jnp.zeros((HD, block), F32)
        grad_value = jnp.zeros((HD, block), F32)
        for row in range(col, 2 * SLOTS):
            query, grad_row = part(0, row), tokens(grad_attn, row)
            probs = jnp.exp2(dot(key, query, 0, 0) * factor - lse[pl.ds(row, 1), :])
            if row == col:
                probs = jnp.where(mask, probs, 0.0)
            grad_probs = dot(value, grad_row, 0, 0)
            grad_scores = (probs * (grad_probs - delta[pl.ds(row, 1), :])).astype(BF16)
            grad_value = grad_value + dot(grad_row, probs.astype(BF16), 1, 1)
            grad_key = grad_key + dot(query, grad_scores, 1, 1)
            term = dot(key, grad_scores, 1, 0)
            if col == 0:
                grad_q[row] = term
            else:
                grad_q[row] += term
        where = ((col % SLOTS) ^ me, pl.ds((col // SLOTS) * block, block))
        out[where[0], 1, :, where[1]] = (grad_key * SCALE).astype(BF16)
        out[where[0], 2, :, where[1]] = grad_value.astype(BF16)
    for row in range(2 * SLOTS):
        where = ((row % SLOTS) ^ me, pl.ds((row // SLOTS) * block, block))
        out[where[0], 0, :, where[1]] = (grad_q[row] * SCALE).astype(BF16)


def head_spec(width):
    return pl.BlockSpec((SLOTS, None, HD, width), lambda h, me: (0, h, 0, 0))


def triple_spec(width):
    return pl.BlockSpec((SLOTS, 3, None, HD, width), lambda h, me: (0, 0, h, 0, 0))


def attend(me, qkv):
    heads, width = qkv.shape[2], qkv.shape[4]
    block = width // 2
    length = SLOTS * width
    return pl.pallas_call(
        functools.partial(forward_kernel, block),
        out_shape=(
            jax.ShapeDtypeStruct((SLOTS, heads, HD, width), BF16),
            jax.ShapeDtypeStruct((heads, 2 * SLOTS, block), F32),
        ),
        grid_spec=pltpu.PrefetchScalarGridSpec(
            num_scalar_prefetch=1,
            grid=(heads,),
            in_specs=[triple_spec(width)],
            out_specs=(
                head_spec(width),
                pl.BlockSpec((None, 2 * SLOTS, block), lambda h, me: (h, 0, 0)),
            ),
            scratch_shapes=[pltpu.VMEM((length, block), F32)] * 2,
        ),
        compiler_params=pltpu.CompilerParams(vmem_limit_bytes=VMEM_LIMIT),
        cost_estimate=pl.CostEstimate(
            flops=2 * heads * length * length * HD,
            bytes_accessed=8 * heads * HD * length,
            transcendentals=heads * length * length // 2,
        ),
        name="attend",
    )(me, qkv)


def attend_back(me, qkv, attn, grad_attn, lse):
    heads, width = qkv.shape[2], qkv.shape[4]
    block = width // 2
    length = SLOTS * width
    return pl.pallas_call(
        functools.partial(backward_kernel, block),
        out_shape=jax.ShapeDtypeStruct(qkv.shape, BF16),
        grid_spec=pltpu.PrefetchScalarGridSpec(
            num_scalar_prefetch=1,
            grid=(heads,),
            in_specs=[
                triple_spec(width),
                head_spec(width),
                head_spec(width),
                pl.BlockSpec((None, 2 * SLOTS, block), lambda h, me: (h, 0, 0)),
            ],
            out_specs=triple_spec(width),
            scratch_shapes=[
                pltpu.VMEM((2 * SLOTS, HD, block), F32),
                pltpu.VMEM((2 * SLOTS, block), F32),
            ],
        ),
        compiler_params=pltpu.CompilerParams(vmem_limit_bytes=VMEM_LIMIT),
        cost_estimate=pl.CostEstimate(
            flops=5 * heads * length * length * HD,
            bytes_accessed=16 * heads * HD * length,
            transcendentals=heads * length * length // 2,
        ),
        name="attend_back",
    )(me, qkv, attn, grad_attn, lse)


def to_attention(slots, head):
    count, features, width = slots.shape
    if count == SLOTS:
        return head.reshape(1), slots
    order = jnp.arange(count) ^ head
    natural = slots[order].reshape(count, features, 2, width // 2)
    tokens = natural.transpose(1, 2, 0, 3).reshape(features, 2, SLOTS, -1)
    return jnp.zeros((1,), jnp.int32), tokens.transpose(2, 0, 1, 3).reshape(SLOTS, features, -1)


def from_attention(tokens, head, count):
    if count == SLOTS:
        return tokens
    features = tokens.shape[1]
    natural = tokens.reshape(SLOTS, features, 2, -1).transpose(1, 2, 0, 3)
    natural = natural.reshape(features, 2, count, -1).transpose(2, 0, 1, 3)
    return natural.reshape(count, features, -1)[jnp.arange(count) ^ head]


def on_device(
    stream_in,
    ln1_gain,
    ln1_bias,
    w_qkv,
    b_qv,
    w_out,
    b_out,
    ln2_gain,
    ln2_bias,
    w_fc,
    b_fc,
    w_proj,
    b_proj,
    cotangent,
):
    seq_dev, tok_rows, width = stream_in.shape
    rows = seq_dev * tok_rows
    dp_count, head_count = lax.axis_size("dp"), lax.axis_size("head")
    devices = dp_count * 2 * head_count
    grid = (dp_count, 2, head_count)
    dp, core, head = lax.axis_index("dp"), lax.axis_index("blk"), lax.axis_index("head")
    ids = jnp.stack([dp, core, head]).astype(jnp.int32)
    group = width // head_count
    heads = group // HD
    own_rows = w_qkv.shape[0]
    hidden_width = w_fc.shape[1]

    sizes = [own_rows] * 8 + [b_fc.shape[0]]
    small = jnp.concatenate(
        [ln1_gain, ln1_bias, b_qv[0], b_qv[1], b_out, ln2_gain, ln2_bias, b_proj, b_fc]
    ).astype(F32)
    small = gather_small(small, ids)
    edges = [sum(sizes[:i]) for i in range(len(sizes) + 1)]
    full = [small[:, edges[i] : edges[i + 1]].reshape(-1) for i in range(len(sizes))]
    gain_one, bias_one, bias_q, bias_v, bias_out, gain_two, bias_two, bias_proj, bias_fc = full

    stream_rows = stream_in.reshape(rows, width)
    normed_one, inv_one = normalize(stream_rows)
    act_one = (normed_one * gain_one + bias_one).astype(BF16).reshape(seq_dev, tok_rows, width)

    columns = w_qkv.reshape(own_rows, 3, head_count, group)
    parts = [
        pick(columns, head ^ slot, 2).reshape(own_rows, 3 * group) for slot in range(head_count)
    ]
    parts = [parts[0]] + [to_xor(parts[slot], slot) for slot in range(1, head_count)]
    shard = jnp.stack(parts)
    theirs_z = gather_z(shard)
    core_z = to_other_core(theirs_z)
    group_w = place(
        [theirs_z[:, slot] for slot in range(head_count)]
        + [core_z[:, slot] for slot in range(head_count)],
        ids,
    ).reshape(width, 3 * group)

    own_half = by_half(core, pick(act_one, core), to_other_core(pick(act_one, 1 - core)))
    own_half = own_half.reshape(2 * tok_rows, width)
    acts = gather_plane(own_half)
    qkv_bias = jnp.concatenate(
        [
            pick(bias_q.reshape(head_count, group), head),
            jnp.zeros((group,), F32),
            pick(bias_v.reshape(head_count, group), head),
        ]
    )[:, None]
    qkv_slots = jnp.stack([(dot(group_w, act, 0, 1) + qkv_bias).astype(BF16) for act in acts])
    me, qkv = to_attention(qkv_slots, head)
    qkv = qkv.reshape(SLOTS, 3, heads, HD, -1)
    attn, lse = attend(me, qkv)

    full_wout = gather_rows(w_out, ids).reshape(width, width)
    full_wfc = gather_rows(w_fc, ids).reshape(width, hidden_width)
    full_wproj = gather_rows(w_proj, ids).reshape(hidden_width, width)

    attn_slots = from_attention(attn.reshape(SLOTS, group, -1), head, head_count)
    attn_all = jnp.zeros((head_count, group, 2 * tok_rows), BF16)
    for slot in range(head_count):
        piece = attn_slots[slot]
        piece = to_xor(piece, slot) if slot else piece
        attn_all = lax.dynamic_update_index_in_dim(attn_all, piece, head ^ slot, 0)
    attn_all = attn_all.reshape(width, 2, tok_rows)
    attn_all = attn_all.reshape(width, 2 * tok_rows)
    first, second = attn_all[:, :tok_rows], attn_all[:, tok_rows:]
    keep = jnp.where(core == 0, first, second)
    away = jnp.where(core == 0, second, first)
    attn_cols = by_half(core, keep, to_other_core(away))

    resid = (
        stream_rows
        + jnp.einsum("sdt,de->ste", attn_cols, full_wout, preferred_element_type=F32).reshape(
            rows, width
        )
        + bias_out
    )
    normed_two, inv_two = normalize(resid)
    ctx = (normed_two * gain_two + bias_two).astype(BF16)
    pre_act = dot(ctx, full_wfc, 1, 0) + bias_fc
    gelu_val, gelu_slope = gelu_pair(pre_act)
    hidden = gelu_val.astype(BF16)
    stream_out = resid + dot(hidden, full_wproj, 1, 0) + bias_proj

    cot_rows = cotangent.reshape(rows, width)
    cot_low = cot_rows.astype(BF16)
    grad_b_proj = jnp.sum(cot_rows, axis=0)
    grad_w_proj = dot(hidden, cot_low, 0, 0).astype(BF16)
    grad_pre = dot(cot_low, full_wproj, 1, 1) * gelu_slope
    grad_b_fc = jnp.sum(grad_pre, axis=0)
    pre_low = grad_pre.astype(BF16)
    grad_w_fc = dot(ctx, pre_low, 0, 0).astype(BF16)
    grad_ctx = dot(pre_low, full_wfc, 1, 1)
    grad_ln2_gain = jnp.sum(grad_ctx * normed_two, axis=0)
    grad_ln2_bias = jnp.sum(grad_ctx, axis=0)
    grad_resid = cot_rows + norm_back(grad_ctx * gain_two, normed_two, inv_two)
    grad_b_out = jnp.sum(grad_resid, axis=0)
    resid_low = grad_resid.astype(BF16)
    resid_three = resid_low.reshape(seq_dev, tok_rows, width)
    grad_w_out = jnp.einsum(
        "sdt,ste->de", attn_cols, resid_three, preferred_element_type=F32
    ).astype(BF16)
    grad_attn_cols = jnp.einsum(
        "ste,de->sdt", resid_three, full_wout, preferred_element_type=F32
    ).astype(BF16)

    shard_wproj = scatter_rows(grad_w_proj.reshape(grid + (-1, width)), core, head, dp)
    shard_wfc = scatter_rows(grad_w_fc.reshape(grid + (-1, hidden_width)), core, head, dp)
    shard_wout = scatter_rows(grad_w_out.reshape(grid + (-1, width)), core, head, dp)

    kept = pick(grad_attn_cols, core)
    arrived = to_other_core(pick(grad_attn_cols, 1 - core))
    grad_half = jnp.where(
        core == 0,
        jnp.concatenate([kept, arrived], axis=1),
        jnp.concatenate([arrived, kept], axis=1),
    ).reshape(head_count, group, 2 * tok_rows)
    grad_slots = jnp.stack(
        [pick(grad_half, head)]
        + [to_xor(pick(grad_half, head ^ slot), slot) for slot in range(1, head_count)]
    )
    _, grad_attn = to_attention(grad_slots, head)
    grad_attn = grad_attn.reshape(SLOTS, heads, HD, -1)
    grad_qkv = attend_back(me, qkv, attn, grad_attn, lse)
    grad_qkv = from_attention(grad_qkv.reshape(SLOTS, 3 * group, -1), head, head_count)

    grad_act_slots = [
        dot(grad_qkv[slot], group_w, 0, 1).astype(BF16) for slot in range(head_count)
    ]
    sums = grad_act_slots[0].astype(F32)
    for slot in range(1, head_count):
        sums = sums + to_xor(grad_act_slots[slot], slot).astype(F32)
    sums = sums.reshape(2, tok_rows, width)
    grad_act = by_half(
        core, pick(sums, core), to_other_core(pick(sums, 1 - core))
    ).reshape(rows, width)

    grad_group_w = dot(acts[0], grad_qkv[0], 0, 1)
    for slot in range(1, head_count):
        grad_group_w = grad_group_w + dot(acts[slot], grad_qkv[slot], 0, 1)
    grad_group_w = grad_group_w.astype(BF16).reshape(grid + (own_rows, 3 * group))
    half_w = pick(grad_group_w, core, 1).astype(F32) + to_other_core(
        pick(grad_group_w, 1 - core, 1)
    ).astype(F32)
    half_low = half_w.astype(BF16)
    shard_w = pick(half_w, dp)
    for step in range(1, dp_count):
        shard_w = shard_w + to_shift(pick(half_low, lax.rem(dp + step, dp_count)), step).astype(F32)
    shard_wqkv = jnp.zeros((own_rows, 3, head_count, group), F32)
    for slot in range(head_count):
        piece = pick(shard_w, head ^ slot)
        piece = to_xor(piece, slot) if slot else piece
        shard_wqkv = lax.dynamic_update_index_in_dim(
            shard_wqkv, piece.reshape(own_rows, 3, group), head ^ slot, 2
        )
    shard_wqkv = shard_wqkv.reshape(own_rows, 3 * width)

    token_sums = jnp.sum(grad_qkv.astype(F32), axis=(0, 2)).reshape(3, group)
    grad_bias = jnp.zeros((3, head_count, group), F32)
    grad_bias = lax.dynamic_update_index_in_dim(grad_bias, token_sums, head, 1).reshape(3, width)

    grad_ln1_gain = jnp.sum(grad_act * normed_one, axis=0)
    grad_ln1_bias = jnp.sum(grad_act, axis=0)
    grad_rows_in = grad_resid + norm_back(grad_act * gain_one, normed_one, inv_one)

    vectors = [
        grad_ln1_gain,
        grad_ln1_bias,
        grad_bias[0],
        grad_bias[2],
        grad_b_out,
        grad_ln2_gain,
        grad_ln2_bias,
        grad_b_proj,
        grad_b_fc,
    ]
    packed = jnp.concatenate([v.reshape(devices, -1) for v in vectors], axis=1)
    mine = scatter_small(packed.reshape(grid + (-1,)), core, head, dp)
    cut = [mine[edges[i] : edges[i + 1]] for i in range(len(sizes))]
    return (
        stream_out.reshape(seq_dev, tok_rows, width),
        grad_rows_in.reshape(seq_dev, tok_rows, width),
        cut[0],
        cut[1],
        shard_wqkv,
        jnp.stack([cut[2], cut[3]]),
        shard_wout.reshape(-1, width),
        cut[4],
        cut[5],
        cut[6],
        shard_wfc.reshape(-1, hidden_width),
        cut[8],
        shard_wproj.reshape(-1, width),
        cut[7],
    )


def solution(mesh):
    every = ("dp", "blk", "head")
    tokens = P("dp", ("blk", "head"), None)
    vector, matrix = P(every), P(every, None)
    in_specs = (
        tokens,
        vector,
        vector,
        matrix,
        P(None, every),
        matrix,
        vector,
        vector,
        vector,
        matrix,
        vector,
        matrix,
        vector,
        tokens,
    )
    out_specs = (
        tokens,
        tokens,
        vector,
        vector,
        matrix,
        P(None, every),
        matrix,
        vector,
        vector,
        vector,
        matrix,
        vector,
        matrix,
        vector,
    )
    return jax.shard_map(
        on_device, mesh=mesh, in_specs=in_specs, out_specs=out_specs, check_vma=False
    )
```

```python
import functools
import math

import jax
import jax.numpy as jnp
from jax import lax
from jax.experimental import pallas as pl
from jax.experimental.pallas import tpu as pltpu
from jax.sharding import PartitionSpec as P

HD = 64
EPSILON = 1e-05
GELU_COEF = 0.044715
ROOT_TWO_PI = math.sqrt(2.0 / math.pi)
SCALE = 1.0 / math.sqrt(HD)
LOG2E = math.log2(math.e)
F32 = jnp.float32
BF16 = jnp.bfloat16
VMEM_LIMIT = 48 * 1024 * 1024


def normalize(stream):
    centred = stream - jnp.mean(stream, axis=-1, keepdims=True)
    inv_std = lax.rsqrt(jnp.mean(centred * centred, axis=-1, keepdims=True) + EPSILON)
    return (centred * inv_std, inv_std)


def norm_back(grad_normed, normed, inv_std):
    return inv_std * (
        grad_normed
        - jnp.mean(grad_normed, axis=-1, keepdims=True)
        - normed * jnp.mean(grad_normed * normed, axis=-1, keepdims=True)
    )


def gelu_pair(pre_act):
    tangent = jnp.tanh(ROOT_TWO_PI * (pre_act + GELU_COEF * pre_act * pre_act * pre_act))
    value = 0.5 * pre_act * (1.0 + tangent)
    slope = 0.5 * (1.0 + tangent) + 0.5 * pre_act * (1.0 - tangent * tangent) * ROOT_TWO_PI * (
        1.0 + 3.0 * GELU_COEF * pre_act * pre_act
    )
    return (value, slope)


def dot(left, right, left_dim, right_dim):
    return lax.dot_general(
        left, right, (((left_dim,), (right_dim,)), ((), ())), preferred_element_type=F32
    )


def to_xor(value, step):
    count = lax.axis_size("head")
    return lax.ppermute(value, "head", [(i, i ^ step) for i in range(count)])


def to_shift(value, step):
    count = lax.axis_size("dp")
    return lax.ppermute(value, "dp", [(i, (i + step) % count) for i in range(count)])


def to_other_core(value):
    return lax.ppermute(value, "blk", [(0, 1), (1, 0)])


def pick(stacked, index, axis=0):
    return lax.dynamic_index_in_dim(stacked, index, axis, keepdims=False)


def by_half(core, own, other):
    return jnp.where(core == 0, jnp.stack([own, other]), jnp.stack([other, own]))


def place_kernel(widths, ids, *refs):
    count = (len(refs) - 1 - len(widths)) // 2
    pieces, outs, sem = refs[: 2 * count], refs[2 * count : -1], refs[-1]
    core, head = ids[1], ids[2]
    copies = []
    for which in range(2):
        for slot in range(count):
            start = 0
            for out, columns in zip(outs, widths):
                copies.append(
                    pltpu.make_async_copy(
                        pieces[which * count + slot].at[:, :, pl.ds(start, columns)],
                        out.at[:, core ^ which, head ^ slot],
                        sem.at[len(copies)],
                    )
                )
                start += columns
    for copy in copies:
        copy.start()
    for copy in copies:
        copy.wait()


def place(mine, widths, ids):
    dp_count, rows, _ = mine[0].shape
    pieces = list(mine) + [to_other_core(piece) for piece in mine]
    shapes = [(dp_count, 2, len(mine), rows, columns) for columns in widths]
    outs = pl.pallas_call(
        functools.partial(place_kernel, widths),
        out_shape=[jax.ShapeDtypeStruct(shape, BF16) for shape in shapes],
        grid_spec=pltpu.PrefetchScalarGridSpec(
            num_scalar_prefetch=1,
            grid=(1,),
            in_specs=[pl.BlockSpec(memory_space=pl.ANY)] * len(pieces),
            out_specs=[
                pl.BlockSpec(
                    shape, lambda i, ids: (0, 0, 0, 0, 0), pipeline_mode=pl.Buffered(1)
                )
                for shape in shapes
            ],
            scratch_shapes=[pltpu.SemaphoreType.DMA((len(pieces) * len(widths),))],
        ),
        compiler_params=pltpu.CompilerParams(vmem_limit_bytes=VMEM_LIMIT),
        name="place",
    )(ids, *pieces)
    return [out.reshape(-1, columns) for out, columns in zip(outs, widths)]


def gather_dp(shard):
    full = lax.all_gather(shard, "dp", axis=0, tiled=True)
    return full.reshape((-1,) + shard.shape)


def split_terms(grad, core):
    return (
        pick(grad, core, 1).transpose(1, 0, 2, 3),
        pick(grad, 1 - core, 1).transpose(1, 0, 2, 3),
    )


def chip_terms(own, away):
    total = (own.astype(F32) + to_other_core(away).astype(F32)).astype(BF16)
    return total.reshape(-1, total.shape[-1])


def scatter_plane(terms):
    return lax.psum_scatter(terms, "head", scatter_dimension=0, tiled=True)


def scatter_dp(terms):
    return lax.psum_scatter(terms, "dp", scatter_dimension=0, tiled=True).astype(F32)


def gather_z(shard):
    return jnp.stack([shard] + [to_shift(shard, k) for k in range(1, lax.axis_size("dp"))])


def gather_plane(own):
    return [own] + [to_xor(own, j) for j in range(1, lax.axis_size("head"))]


def plane_near(own):
    return to_xor(own, 1), to_xor(own, 2)


def plane_far(own, near, axis):
    half = own.shape[axis] // 2
    lower = to_xor(lax.slice_in_dim(near[0], 0, half, axis=axis), 2)
    upper = to_xor(lax.slice_in_dim(near[1], half, 2 * half, axis=axis), 1)
    return [own, near[0], near[1], jnp.concatenate([lower, upper], axis=axis)]


def sum_far(parts, axis):
    half = parts[3].shape[axis] // 2
    return (
        to_xor(lax.slice_in_dim(parts[3], 0, half, axis=axis), 1),
        to_xor(lax.slice_in_dim(parts[3], half, 2 * half, axis=axis), 2),
    )


def sum_near(parts, arrived, axis):
    half = parts[3].shape[axis] // 2
    cut = lambda value, low: lax.slice_in_dim(value, low, low + half, axis=axis)
    to_y = jnp.concatenate(
        [
            (cut(parts[2], 0).astype(F32) + arrived[0].astype(F32)).astype(BF16),
            cut(parts[2], half),
        ],
        axis=axis,
    )
    to_x = jnp.concatenate(
        [
            cut(parts[1], 0),
            (cut(parts[1], half).astype(F32) + arrived[1].astype(F32)).astype(BF16),
        ],
        axis=axis,
    )
    return to_xor(to_x, 1), to_xor(to_y, 2)


def core_terms(grad, core):
    return to_other_core(pick(grad, 1 - core, 1))


def plane_total(own, terms):
    total = own
    for piece in terms:
        total = total + piece.astype(F32)
    return total


def scatter_z(total, dp):
    dp_count = total.shape[0]
    low = total.astype(BF16)
    result = pick(total, dp)
    for step in range(1, dp_count):
        result = result + to_shift(pick(low, lax.rem(dp + step, dp_count)), step).astype(F32)
    return result


def together(*values):
    return lax.optimization_barrier(values)


def gather_small(vector, ids):
    dp_count, head_count = lax.axis_size("dp"), lax.axis_size("head")
    rows = gather_z(vector[None])
    rows = jnp.stack(gather_plane(rows))
    rows = jnp.stack([rows, to_other_core(rows)])
    total = 2 * head_count * dp_count
    slot = jnp.arange(total)
    which, plane, step = slot // (head_count * dp_count), (slot // dp_count) % head_count, slot % dp_count
    source = ((ids[0] - step) % dp_count) * 2 * head_count + (ids[1] ^ which) * head_count + (ids[2] ^ plane)
    chosen = (source[None, :] == jnp.arange(total)[:, None]).astype(F32)
    return jnp.dot(chosen, rows.reshape(total, -1), precision=lax.Precision.HIGHEST)


def scatter_small(rows, core, head, dp):
    dp_count, _, head_count = rows.shape[:3]
    half = pick(rows, core, 1) + to_other_core(pick(rows, 1 - core, 1))
    total = pick(half, head, 1)
    for slot in range(1, head_count):
        total = total + to_xor(pick(half, head ^ slot, 1), slot)
    result = pick(total, dp)
    for step in range(1, dp_count):
        result = result + to_shift(pick(total, lax.rem(dp + step, dp_count)), step)
    return result


SLOTS = 4


def causal(block):
    key = lax.broadcasted_iota(jnp.int32, (block, block), 0)
    query = lax.broadcasted_iota(jnp.int32, (block, block), 1)
    return key <= query


def forward_kernel(block, me_ref, qkv, out, lse, scores_a, scores_b):
    me = me_ref[0]
    factor = SCALE * LOG2E
    mask = causal(block)

    def part(which, pos):
        return qkv[(pos % SLOTS) ^ me, which, :, pl.ds((pos // SLOTS) * block, block)]

    for row in range(2 * SLOTS):
        scores = scores_a if row % 2 == 0 else scores_b
        query = part(0, row)
        top = None
        for col in range(row + 1):
            tile = dot(part(1, col), query, 0, 0)
            if col == row:
                tile = jnp.where(mask, tile, -jnp.inf)
            scores[pl.ds(col * block, block), :] = tile
            high = jnp.max(tile, axis=0, keepdims=True)
            top = high if top is None else jnp.maximum(top, high)
        shift = top * factor
        total = jnp.zeros_like(top)
        result = jnp.zeros((HD, block), F32)
        for col in range(row + 1):
            probs = jnp.exp2(scores[pl.ds(col * block, block), :] * factor - shift)
            total = total + jnp.sum(probs, axis=0, keepdims=True)
            result = result + dot(part(2, col), probs.astype(BF16), 1, 0)
        out[(row % SLOTS) ^ me, :, pl.ds((row // SLOTS) * block, block)] = (result / total).astype(BF16)
        lse[pl.ds(row, 1), :] = shift + jnp.log2(total)


def backward_kernel(block, me_ref, qkv, attn, grad_attn, lse, out, grad_q, delta):
    me = me_ref[0]
    factor = SCALE * LOG2E
    mask = causal(block)

    def part(which, pos):
        return qkv[(pos % SLOTS) ^ me, which, :, pl.ds((pos // SLOTS) * block, block)]

    def tokens(ref, pos):
        return ref[(pos % SLOTS) ^ me, :, pl.ds((pos // SLOTS) * block, block)]

    for row in range(2 * SLOTS):
        product = tokens(grad_attn, row).astype(F32) * tokens(attn, row).astype(F32)
        delta[pl.ds(row, 1), :] = jnp.sum(product, axis=0, keepdims=True)
    for col in range(2 * SLOTS):
        key, value = part(1, col), part(2, col)
        grad_key = jnp.zeros((HD, block), F32)
        grad_value = jnp.zeros((HD, block), F32)
        for row in range(col, 2 * SLOTS):
            query, grad_row = part(0, row), tokens(grad_attn, row)
            probs = jnp.exp2(dot(key, query, 0, 0) * factor - lse[pl.ds(row, 1), :])
            if row == col:
                probs = jnp.where(mask, probs, 0.0)
            grad_probs = dot(value, grad_row, 0, 0)
            grad_scores = (probs * (grad_probs - delta[pl.ds(row, 1), :])).astype(BF16)
            grad_value = grad_value + dot(grad_row, probs.astype(BF16), 1, 1)
            grad_key = grad_key + dot(query, grad_scores, 1, 1)
            term = dot(key, grad_scores, 1, 0)
            if col == 0:
                grad_q[row] = term
            else:
                grad_q[row] += term
        where = ((col % SLOTS) ^ me, pl.ds((col // SLOTS) * block, block))
        out[where[0], 1, :, where[1]] = (grad_key * SCALE).astype(BF16)
        out[where[0], 2, :, where[1]] = grad_value.astype(BF16)
    for row in range(2 * SLOTS):
        where = ((row % SLOTS) ^ me, pl.ds((row // SLOTS) * block, block))
        out[where[0], 0, :, where[1]] = (grad_q[row] * SCALE).astype(BF16)


def head_spec(width):
    return pl.BlockSpec((SLOTS, None, HD, width), lambda h, me: (0, h, 0, 0))


def triple_spec(width):
    return pl.BlockSpec((SLOTS, 3, None, HD, width), lambda h, me: (0, 0, h, 0, 0))


def attend(me, qkv):
    heads, width = qkv.shape[2], qkv.shape[4]
    block = width // 2
    length = SLOTS * width
    return pl.pallas_call(
        functools.partial(forward_kernel, block),
        out_shape=(
            jax.ShapeDtypeStruct((SLOTS, heads, HD, width), BF16),
            jax.ShapeDtypeStruct((heads, 2 * SLOTS, block), F32),
        ),
        grid_spec=pltpu.PrefetchScalarGridSpec(
            num_scalar_prefetch=1,
            grid=(heads,),
            in_specs=[triple_spec(width)],
            out_specs=(
                head_spec(width),
                pl.BlockSpec((None, 2 * SLOTS, block), lambda h, me: (h, 0, 0)),
            ),
            scratch_shapes=[pltpu.VMEM((length, block), F32)] * 2,
        ),
        compiler_params=pltpu.CompilerParams(vmem_limit_bytes=VMEM_LIMIT),
        cost_estimate=pl.CostEstimate(
            flops=2 * heads * length * length * HD,
            bytes_accessed=8 * heads * HD * length,
            transcendentals=heads * length * length // 2,
        ),
        name="attend",
    )(me, qkv)


def attend_back(me, qkv, attn, grad_attn, lse):
    heads, width = qkv.shape[2], qkv.shape[4]
    block = width // 2
    length = SLOTS * width
    return pl.pallas_call(
        functools.partial(backward_kernel, block),
        out_shape=jax.ShapeDtypeStruct(qkv.shape, BF16),
        grid_spec=pltpu.PrefetchScalarGridSpec(
            num_scalar_prefetch=1,
            grid=(heads,),
            in_specs=[
                triple_spec(width),
                head_spec(width),
                head_spec(width),
                pl.BlockSpec((None, 2 * SLOTS, block), lambda h, me: (h, 0, 0)),
            ],
            out_specs=triple_spec(width),
            scratch_shapes=[
                pltpu.VMEM((2 * SLOTS, HD, block), F32),
                pltpu.VMEM((2 * SLOTS, block), F32),
            ],
        ),
        compiler_params=pltpu.CompilerParams(vmem_limit_bytes=VMEM_LIMIT),
        cost_estimate=pl.CostEstimate(
            flops=5 * heads * length * length * HD,
            bytes_accessed=16 * heads * HD * length,
            transcendentals=heads * length * length // 2,
        ),
        name="attend_back",
    )(me, qkv, attn, grad_attn, lse)


def feed_kernel(ctx, weight, bias, hidden, slope):
    pre = dot(ctx[...], weight[...], 1, 0) + bias[...]
    value, steep = gelu_pair(pre)
    hidden[...] = value.astype(BF16)
    slope[...] = steep


def feed(ctx, weight, bias):
    rows, width = ctx.shape
    units = weight.shape[1]
    block = min(512, units)
    return pl.pallas_call(
        feed_kernel,
        out_shape=(
            jax.ShapeDtypeStruct((rows, units), BF16),
            jax.ShapeDtypeStruct((rows, units), F32),
        ),
        grid=(units // block,),
        in_specs=[
            pl.BlockSpec((rows, width), lambda i: (0, 0)),
            pl.BlockSpec((width, block), lambda i: (0, i)),
            pl.BlockSpec((1, block), lambda i: (0, i)),
        ],
        out_specs=(
            pl.BlockSpec((rows, block), lambda i: (0, i)),
            pl.BlockSpec((rows, block), lambda i: (0, i)),
        ),
        compiler_params=pltpu.CompilerParams(vmem_limit_bytes=VMEM_LIMIT),
        cost_estimate=pl.CostEstimate(
            flops=2 * rows * width * units,
            bytes_accessed=2 * width * units + 6 * rows * units,
            transcendentals=rows * units,
        ),
        name="feed",
    )(ctx, weight, bias.reshape(1, -1))


def feed_back_kernel(
    cot, hidden, slope, w_fc, w_proj, base, pre_low, grad_bias, grad_ctx, stream, sum_ctx, sum_out
):
    step = pl.program_id(0)
    grad_pre = dot(cot[...], w_proj[...], 1, 1) * slope[...]
    grad_bias[...] = jnp.sum(grad_pre, axis=0, keepdims=True)
    low = grad_pre.astype(BF16)
    pre_low[...] = low
    back = dot(low, w_fc[...], 1, 1)
    ahead = dot(hidden[...], w_proj[...], 1, 0)

    @pl.when(step == 0)
    def _():
        sum_ctx[...] = back
        sum_out[...] = base[...] + ahead

    @pl.when(step > 0)
    def _():
        sum_ctx[...] += back
        sum_out[...] += ahead

    @pl.when(step == pl.num_programs(0) - 1)
    def _():
        grad_ctx[...] = sum_ctx[...]
        stream[...] = sum_out[...]


def feed_back(cot, hidden, slope, w_fc, w_proj, base):
    rows, width = cot.shape
    units = hidden.shape[1]
    block = min(512, units)
    whole = pl.BlockSpec((rows, width), lambda i: (0, 0))
    columns = pl.BlockSpec((rows, block), lambda i: (0, i))
    return pl.pallas_call(
        feed_back_kernel,
        out_shape=(
            jax.ShapeDtypeStruct((rows, units), BF16),
            jax.ShapeDtypeStruct((1, units), F32),
            jax.ShapeDtypeStruct((rows, width), F32),
            jax.ShapeDtypeStruct((rows, width), F32),
        ),
        grid=(units // block,),
        in_specs=[
            whole,
            columns,
            columns,
            pl.BlockSpec((width, block), lambda i: (0, i)),
            pl.BlockSpec((block, width), lambda i: (i, 0)),
            whole,
        ],
        out_specs=(columns, pl.BlockSpec((1, block), lambda i: (0, i)), whole, whole),
        scratch_shapes=[pltpu.VMEM((rows, width), F32)] * 2,
        compiler_params=pltpu.CompilerParams(vmem_limit_bytes=VMEM_LIMIT),
        cost_estimate=pl.CostEstimate(
            flops=6 * rows * width * units,
            bytes_accessed=4 * width * units + 8 * rows * units,
            transcendentals=0,
        ),
        name="feed_back",
    )(cot, hidden, slope, w_fc, w_proj, base)


def split_rows(core, value, own, away):
    count, rows = own.shape[0], own.shape[2]
    value = value.astype(BF16)
    half = count * rows
    first = value[:half].reshape(count, 1, rows, -1)
    second = value[half:].reshape(count, 1, rows, -1)

    @pl.when(core == 0)
    def _():
        own[...] = first
        away[...] = second

    @pl.when(core == 1)
    def _():
        own[...] = second
        away[...] = first


def weight_kernel(ids, left, right, own, away):
    split_rows(ids[1], dot(left[...], right[...], 0, 0), own, away)


def weight_pair_kernel(ids, left, right, attn, resid, own, away):
    units = right.shape[1]
    total = dot(attn[0], resid[0], 1, 0)
    for seq in range(1, attn.shape[0]):
        total = total + dot(attn[seq], resid[seq], 1, 0)
    split_rows(ids[1], dot(left[...], right[...], 0, 0), own.at[..., pl.ds(0, units)], away.at[..., pl.ds(0, units)])
    split_rows(ids[1], total, own.at[..., pl.ds(units, total.shape[1])], away.at[..., pl.ds(units, total.shape[1])])


def weight_call(kernel, counts, rows, columns, in_specs, flops, name):
    dp_count, head_count = counts
    spec = pl.BlockSpec((head_count, 1, rows, columns), lambda d, ids: (0, d, 0, 0))
    shape = jax.ShapeDtypeStruct((head_count, dp_count, rows, columns), BF16)
    return pl.pallas_call(
        kernel,
        out_shape=(shape, shape),
        grid_spec=pltpu.PrefetchScalarGridSpec(
            num_scalar_prefetch=1, grid=(dp_count,), in_specs=in_specs, out_specs=(spec, spec)
        ),
        compiler_params=pltpu.CompilerParams(vmem_limit_bytes=VMEM_LIMIT),
        cost_estimate=pl.CostEstimate(
            flops=flops, bytes_accessed=4 * head_count * dp_count * rows * columns, transcendentals=0
        ),
        name=name,
    )


def weight_terms(ids, left, right, counts, rows):
    tokens, columns = right.shape
    span = 2 * counts[1] * rows
    return weight_call(
        weight_kernel,
        counts,
        rows,
        columns,
        [
            pl.BlockSpec((tokens, span), lambda d, ids: (0, d)),
            pl.BlockSpec((tokens, columns), lambda d, ids: (0, 0)),
        ],
        2 * tokens * columns * left.shape[1],
        "weight_terms",
    )(ids, left, right)


def weight_pair_terms(ids, left, right, attn, resid, counts, rows):
    tokens, units = right.shape
    seqs, _, features, seq_tokens = attn.shape
    width = resid.shape[2]
    span = 2 * counts[1] * rows
    return weight_call(
        weight_pair_kernel,
        counts,
        rows,
        units + width,
        [
            pl.BlockSpec((tokens, span), lambda d, ids: (0, d)),
            pl.BlockSpec((tokens, units), lambda d, ids: (0, 0)),
            pl.BlockSpec((seqs, None, features, seq_tokens), lambda d, ids: (0, d ^ ids[2], 0, 0)),
            pl.BlockSpec(resid.shape, lambda d, ids: (0, 0, 0)),
        ],
        2 * tokens * (units + width) * left.shape[1],
        "weight_pair_terms",
    )(ids, left, right, attn, resid)


def to_attention(slots, head):
    count, features, width = slots.shape
    if count == SLOTS:
        return head.reshape(1), slots
    order = jnp.arange(count) ^ head
    natural = slots[order].reshape(count, features, 2, width // 2)
    tokens = natural.transpose(1, 2, 0, 3).reshape(features, 2, SLOTS, -1)
    return jnp.zeros((1,), jnp.int32), tokens.transpose(2, 0, 1, 3).reshape(SLOTS, features, -1)


def from_attention(tokens, head, count):
    if count == SLOTS:
        return tokens
    features = tokens.shape[1]
    natural = tokens.reshape(SLOTS, features, 2, -1).transpose(1, 2, 0, 3)
    natural = natural.reshape(features, 2, count, -1).transpose(2, 0, 1, 3)
    return natural.reshape(count, features, -1)[jnp.arange(count) ^ head]


def on_device(
    stream_in,
    ln1_gain,
    ln1_bias,
    w_qkv,
    b_qv,
    w_out,
    b_out,
    ln2_gain,
    ln2_bias,
    w_fc,
    b_fc,
    w_proj,
    b_proj,
    cotangent,
):
    seq_dev, tok_rows, width = stream_in.shape
    rows = seq_dev * tok_rows
    dp_count, head_count = lax.axis_size("dp"), lax.axis_size("head")
    devices = dp_count * 2 * head_count
    grid = (dp_count, 2, head_count)
    dp, core, head = lax.axis_index("dp"), lax.axis_index("blk"), lax.axis_index("head")
    ids = jnp.stack([dp, core, head]).astype(jnp.int32)
    group = width // head_count
    heads = group // HD
    own_rows = w_qkv.shape[0]
    hidden_width = w_fc.shape[1]

    sizes = [own_rows] * 8 + [b_fc.shape[0]]
    small = jnp.concatenate(
        [ln1_gain, ln1_bias, b_qv[0], b_qv[1], b_out, ln2_gain, ln2_bias, b_proj, b_fc]
    ).astype(F32)
    small = gather_small(small, ids)
    edges = [sum(sizes[:i]) for i in range(len(sizes) + 1)]
    full = [small[:, edges[i] : edges[i + 1]].reshape(-1) for i in range(len(sizes))]
    gain_one, bias_one, bias_q, bias_v, bias_out, gain_two, bias_two, bias_proj, bias_fc = full

    square = head_count == 4
    stream_rows = stream_in.reshape(rows, width)
    normed_one, inv_one = normalize(stream_rows)
    act_one = (normed_one * gain_one + bias_one).astype(BF16).reshape(seq_dev, tok_rows, width)

    columns = w_qkv.reshape(own_rows, 3, head_count, group)
    parts = [
        pick(columns, head ^ slot, 2).reshape(own_rows, 3 * group) for slot in range(head_count)
    ]
    parts = [parts[0]] + [to_xor(parts[slot], slot) for slot in range(1, head_count)]
    one_z = gather_dp(jnp.concatenate([w_fc, w_out], axis=1))
    two_z = gather_dp(w_proj)

    own_half = by_half(core, pick(act_one, core), to_other_core(pick(act_one, 1 - core)))
    own_half = own_half.reshape(2 * tok_rows, width)
    own_half, shard = together(own_half, jnp.concatenate(parts, axis=1))
    group_z = gather_z(shard)
    group_z = jnp.stack([pick(group_z, (dp + dp_count - k) % dp_count) for k in range(dp_count)])
    wide = 3 * group
    (group_w,) = place(
        [group_z[:, :, slot * wide : (slot + 1) * wide] for slot in range(head_count)],
        (wide,),
        ids,
    )
    acts = plane_far(own_half, plane_near(own_half), 0) if square else gather_plane(own_half)
    *acts, one_z = together(*acts, one_z)
    one_near = plane_near(one_z) if square else gather_plane(one_z)
    qkv_bias = jnp.concatenate(
        [
            pick(bias_q.reshape(head_count, group), head),
            jnp.zeros((group,), F32),
            pick(bias_v.reshape(head_count, group), head),
        ]
    )[:, None]
    qkv_slots = jnp.stack([(dot(group_w, act, 0, 1) + qkv_bias).astype(BF16) for act in acts])
    me, qkv = to_attention(qkv_slots, head)
    qkv = qkv.reshape(SLOTS, 3, heads, HD, -1)
    attn, lse = attend(me, qkv)
    attn, two_z, *one_near = together(attn, two_z, *one_near)
    attn_slots = from_attention(attn.reshape(SLOTS, group, -1), head, head_count)
    attn_all = [attn_slots[0]] + [to_xor(attn_slots[j], j) for j in range(1, head_count)]
    one_pieces = plane_far(one_z, one_near, 2) if square else one_near
    attn_all = jnp.stack(attn_all)
    first, second = attn_all[:, :, :tok_rows], attn_all[:, :, tok_rows:]
    keep = jnp.where(core == 0, first, second)
    away = jnp.where(core == 0, second, first)
    attn_cols = by_half(core, keep, to_other_core(away))

    attn_cols, two_z, *one_pieces = together(attn_cols, two_z, *one_pieces)
    two_near = plane_near(two_z) if square else gather_plane(two_z)
    full_wfc, full_wout = place(one_pieces, (hidden_width, width), ids)
    slot_wout = full_wout.reshape(head_count, group, width)
    slot_wout = jnp.stack([pick(slot_wout, head ^ slot) for slot in range(head_count)])

    resid = (
        stream_rows
        + jnp.einsum("sjdt,jde->ste", attn_cols, slot_wout, preferred_element_type=F32).reshape(
            rows, width
        )
        + bias_out
    )
    normed_two, inv_two = normalize(resid)
    ctx = (normed_two * gain_two + bias_two).astype(BF16)
    ctx, *two_near = together(ctx, *two_near)
    two_pieces = plane_far(two_z, two_near, 1) if square else two_near
    hidden, slope = feed(ctx, full_wfc, bias_fc)
    cot_rows = cotangent.reshape(rows, width)
    cot_low = cot_rows.astype(BF16)
    grad_b_proj = jnp.sum(cot_rows, axis=0)
    chips = (dp_count, head_count)
    aligned = group == 2 * head_count * own_rows and (head_count * own_rows) % 128 == 0
    if aligned:
        two_own, two_away = weight_terms(ids, hidden, cot_low, chips, w_proj.shape[0])
    else:
        two_own, two_away = split_terms(
            dot(hidden, cot_low, 0, 0).astype(BF16).reshape(grid + (-1, width)), core
        )
    two_terms = chip_terms(two_own, two_away)
    (full_wproj,) = place(two_pieces, (width,), ids)
    two_plane = scatter_plane(two_terms)
    pre_low, grad_b_fc, grad_ctx, stream_out = feed_back(
        cot_low, hidden, slope, full_wfc, full_wproj, resid + bias_proj
    )
    grad_b_fc = grad_b_fc.reshape(-1)
    grad_ln2_gain = jnp.sum(grad_ctx * normed_two, axis=0)
    grad_ln2_bias = jnp.sum(grad_ctx, axis=0)
    grad_resid = cot_rows + norm_back(grad_ctx * gain_two, normed_two, inv_two)
    grad_b_out = jnp.sum(grad_resid, axis=0)
    resid_low = grad_resid.astype(BF16)
    resid_three = resid_low.reshape(seq_dev, tok_rows, width)
    grad_attn_cols = jnp.einsum(
        "ste,jde->sjdt", resid_three, slot_wout, preferred_element_type=F32
    ).astype(BF16)
    kept = pick(grad_attn_cols, core)
    arrived = to_other_core(pick(grad_attn_cols, 1 - core))
    grad_half = jnp.where(
        core == 0,
        jnp.concatenate([kept, arrived], axis=2),
        jnp.concatenate([arrived, kept], axis=2),
    )
    grad_slots = [grad_half[0]] + [to_xor(grad_half[j], j) for j in range(1, head_count)]

    if aligned:
        one_own, one_away = weight_pair_terms(
            ids, ctx, pre_low, attn_cols, resid_three, chips, own_rows
        )
    else:
        grad_w_fc = dot(ctx, pre_low, 0, 0).astype(BF16)
        grad_w_out = jnp.einsum(
            "sjdt,ste->jde", attn_cols, resid_three, preferred_element_type=F32
        ).astype(BF16)
        grad_w_out = jnp.stack([pick(grad_w_out, head ^ slot) for slot in range(head_count)])
        one_own, one_away = split_terms(
            jnp.concatenate(
                [
                    grad_w_fc.reshape(grid + (-1, hidden_width)),
                    grad_w_out.reshape(grid + (-1, width)),
                ],
                axis=4,
            ),
            core,
        )
    one_terms = chip_terms(one_own, one_away)
    *grad_slots, one_terms = together(*grad_slots, one_terms)
    one_plane = scatter_plane(one_terms)

    _, grad_attn = to_attention(jnp.stack(grad_slots), head)
    grad_attn = grad_attn.reshape(SLOTS, heads, HD, -1)
    grad_qkv = attend_back(me, qkv, attn, grad_attn, lse)
    grad_qkv = from_attention(grad_qkv.reshape(SLOTS, 3 * group, -1), head, head_count)

    act_parts = [dot(grad_qkv[slot], group_w, 0, 1) for slot in range(head_count)]
    act_parts = [act_parts[0]] + [part.astype(BF16) for part in act_parts[1:]]
    act_far = sum_far(act_parts, 0) if square else []
    grad_qkv, one_plane, two_plane, *act_far = together(grad_qkv, one_plane, two_plane, *act_far)
    both = jnp.concatenate(
        [two_plane.reshape(dp_count, -1, width)]
        + [
            one_plane.reshape(dp_count, own_rows, -1)[:, :, i : i + width]
            for i in range(0, one_plane.shape[1], width)
        ],
        axis=1,
    )
    both, *act_far = together(both, *act_far)
    if square:
        act_terms = sum_near(act_parts, act_far, 0)
    else:
        act_terms = [to_xor(act_parts[j], j) for j in range(1, head_count)]
    sums = plane_total(act_parts[0], act_terms).reshape(2, tok_rows, width)
    grad_act = by_half(
        core, pick(sums, core), to_other_core(pick(sums, 1 - core))
    ).reshape(rows, width)

    both = scatter_dp(both.reshape(-1, width))
    shard_wproj = both[: w_proj.shape[0]]
    columns = both[w_proj.shape[0] :].reshape(-1, own_rows, width)
    shard_wfc = jnp.concatenate([columns[i] for i in range(hidden_width // width)], axis=1)
    shard_wout = columns[-1]

    grad_group_w = dot(acts[0], grad_qkv[0], 0, 1)
    for slot in range(1, head_count):
        grad_group_w = grad_group_w + dot(acts[slot], grad_qkv[slot], 0, 1)
    grad_group_w = grad_group_w.astype(BF16).reshape(grid + (own_rows, 3 * group))
    half_w = pick(grad_group_w, core, 1).astype(F32) + core_terms(grad_group_w, core).astype(F32)
    shard_w = scatter_z(half_w, dp)
    pieces = jnp.stack(
        [pick(shard_w, head)]
        + [to_xor(pick(shard_w, head ^ slot), slot) for slot in range(1, head_count)]
    )
    ordered = [pick(pieces, head ^ slot) for slot in range(head_count)]
    shard_wqkv = jnp.concatenate(
        [piece[:, c * group : (c + 1) * group] for c in range(3) for piece in ordered], axis=1
    )

    token_sums = jnp.sum(grad_qkv.astype(F32), axis=(0, 2)).reshape(3, group)
    grad_bias = jnp.zeros((3, head_count, group), F32)
    grad_bias = lax.dynamic_update_index_in_dim(grad_bias, token_sums, head, 1).reshape(3, width)

    grad_ln1_gain = jnp.sum(grad_act * normed_one, axis=0)
    grad_ln1_bias = jnp.sum(grad_act, axis=0)
    grad_rows_in = grad_resid + norm_back(grad_act * gain_one, normed_one, inv_one)

    vectors = [
        grad_ln1_gain,
        grad_ln1_bias,
        grad_bias[0],
        grad_bias[2],
        grad_b_out,
        grad_ln2_gain,
        grad_ln2_bias,
        grad_b_proj,
        grad_b_fc,
    ]
    packed = jnp.concatenate([v.reshape(devices, -1) for v in vectors], axis=1)
    mine = scatter_small(packed.reshape(grid + (-1,)), core, head, dp)
    cut = [mine[edges[i] : edges[i + 1]] for i in range(len(sizes))]
    return (
        stream_out.reshape(seq_dev, tok_rows, width),
        grad_rows_in.reshape(seq_dev, tok_rows, width),
        cut[0],
        cut[1],
        shard_wqkv,
        jnp.stack([cut[2], cut[3]]),
        shard_wout.reshape(-1, width),
        cut[4],
        cut[5],
        cut[6],
        shard_wfc.reshape(-1, hidden_width),
        cut[8],
        shard_wproj.reshape(-1, width),
        cut[7],
    )


def solution(mesh):
    every = ("dp", "blk", "head")
    tokens = P("dp", ("blk", "head"), None)
    vector, matrix = P(every), P(every, None)
    in_specs = (
        tokens,
        vector,
        vector,
        matrix,
        P(None, every),
        matrix,
        vector,
        vector,
        vector,
        matrix,
        vector,
        matrix,
        vector,
        tokens,
    )
    out_specs = (
        tokens,
        tokens,
        vector,
        vector,
        matrix,
        P(None, every),
        matrix,
        vector,
        vector,
        vector,
        matrix,
        vector,
        matrix,
        vector,
    )
    return jax.shard_map(
        on_device, mesh=mesh, in_specs=in_specs, out_specs=out_specs, check_vma=False
    )
```

```python
import functools
import math

import jax
import jax.numpy as jnp
from jax import lax
from jax.experimental import pallas as pl
from jax.experimental.pallas import tpu as pltpu
from jax.sharding import PartitionSpec as P

HD = 64
EPSILON = 1e-05
GELU_COEF = 0.044715
ROOT_TWO_PI = math.sqrt(2.0 / math.pi)
SCALE = 1.0 / math.sqrt(HD)
LOG2E = math.log2(math.e)
F32 = jnp.float32
BF16 = jnp.bfloat16
VMEM_LIMIT = 48 * 1024 * 1024


def normalize(stream):
    centred = stream - jnp.mean(stream, axis=-1, keepdims=True)
    inv_std = lax.rsqrt(jnp.mean(centred * centred, axis=-1, keepdims=True) + EPSILON)
    return (centred * inv_std, inv_std)


def norm_back(grad_normed, normed, inv_std):
    return inv_std * (
        grad_normed
        - jnp.mean(grad_normed, axis=-1, keepdims=True)
        - normed * jnp.mean(grad_normed * normed, axis=-1, keepdims=True)
    )


def gelu_pair(pre_act):
    square = pre_act * pre_act
    upper = 0.5 + 0.5 * jnp.tanh(pre_act * (ROOT_TWO_PI + (ROOT_TWO_PI * GELU_COEF) * square))
    bend = 2.0 * ROOT_TWO_PI + (6.0 * ROOT_TWO_PI * GELU_COEF) * square
    return (pre_act * upper, upper + upper * (pre_act * (1.0 - upper)) * bend)


def dot(left, right, left_dim, right_dim):
    return lax.dot_general(
        left, right, (((left_dim,), (right_dim,)), ((), ())), preferred_element_type=F32
    )


def to_xor(value, step):
    count = lax.axis_size("head")
    return lax.ppermute(value, "head", [(i, i ^ step) for i in range(count)])


def to_shift(value, step):
    count = lax.axis_size("dp")
    return lax.ppermute(value, "dp", [(i, (i + step) % count) for i in range(count)])


def to_other_core(value):
    return lax.ppermute(value, "blk", [(0, 1), (1, 0)])


def pick(stacked, index, axis=0):
    return lax.dynamic_index_in_dim(stacked, index, axis, keepdims=False)


def by_half(core, own, other):
    return jnp.where(core == 0, jnp.stack([own, other]), jnp.stack([other, own]))


def place_kernel(widths, ids, *refs):
    count = (len(refs) - 1 - len(widths)) // 2
    pieces, outs, sem = refs[: 2 * count], refs[2 * count : -1], refs[-1]
    core, head = ids[1], ids[2]
    copies = []
    for which in range(2):
        for slot in range(count):
            start = 0
            for out, columns in zip(outs, widths):
                copies.append(
                    pltpu.make_async_copy(
                        pieces[which * count + slot].at[:, :, pl.ds(start, columns)],
                        out.at[:, core ^ which, head ^ slot],
                        sem.at[len(copies)],
                    )
                )
                start += columns
    for copy in copies:
        copy.start()
    for copy in copies:
        copy.wait()


def place(mine, widths, ids):
    dp_count, rows, _ = mine[0].shape
    pieces = list(mine) + [to_other_core(piece) for piece in mine]
    shapes = [(dp_count, 2, len(mine), rows, columns) for columns in widths]
    outs = pl.pallas_call(
        functools.partial(place_kernel, widths),
        out_shape=[jax.ShapeDtypeStruct(shape, BF16) for shape in shapes],
        grid_spec=pltpu.PrefetchScalarGridSpec(
            num_scalar_prefetch=1,
            grid=(1,),
            in_specs=[pl.BlockSpec(memory_space=pl.ANY)] * len(pieces),
            out_specs=[
                pl.BlockSpec(
                    shape, lambda i, ids: (0, 0, 0, 0, 0), pipeline_mode=pl.Buffered(1)
                )
                for shape in shapes
            ],
            scratch_shapes=[pltpu.SemaphoreType.DMA((len(pieces) * len(widths),))],
        ),
        compiler_params=pltpu.CompilerParams(vmem_limit_bytes=VMEM_LIMIT),
        name="place",
    )(ids, *pieces)
    return [out.reshape(-1, columns) for out, columns in zip(outs, widths)]


def gather_dp(shard):
    full = lax.all_gather(shard, "dp", axis=0, tiled=True)
    return full.reshape((-1,) + shard.shape)


def split_terms(grad, core):
    return (
        pick(grad, core, 1).transpose(1, 0, 2, 3),
        pick(grad, 1 - core, 1).transpose(1, 0, 2, 3),
    )


def chip_terms(own, away):
    total = (own.astype(F32) + to_other_core(away).astype(F32)).astype(BF16)
    return total.reshape(-1, total.shape[-1])


def scatter_plane(terms):
    return lax.psum_scatter(terms, "head", scatter_dimension=0, tiled=True)


def scatter_dp(terms):
    return lax.psum_scatter(terms, "dp", scatter_dimension=0, tiled=True).astype(F32)


def gather_z(shard):
    return jnp.stack([shard] + [to_shift(shard, k) for k in range(1, lax.axis_size("dp"))])


def gather_plane(own):
    return [own] + [to_xor(own, j) for j in range(1, lax.axis_size("head"))]


def plane_near(own):
    return to_xor(own, 1), to_xor(own, 2)


def plane_far(own, near, axis):
    half = own.shape[axis] // 2
    lower = to_xor(lax.slice_in_dim(near[0], 0, half, axis=axis), 2)
    upper = to_xor(lax.slice_in_dim(near[1], half, 2 * half, axis=axis), 1)
    return [own, near[0], near[1], jnp.concatenate([lower, upper], axis=axis)]


def core_terms(grad, core):
    return to_other_core(pick(grad, 1 - core, 1))


def plane_total(own, terms):
    total = own
    for piece in terms:
        total = total + piece.astype(F32)
    return total


def scatter_z(total, dp):
    dp_count = total.shape[0]
    low = total.astype(BF16)
    result = pick(total, dp)
    for step in range(1, dp_count):
        result = result + to_shift(pick(low, lax.rem(dp + step, dp_count)), step).astype(F32)
    return result


def together(*values):
    return lax.optimization_barrier(values)


def gather_small(vector, ids):
    dp_count, head_count = lax.axis_size("dp"), lax.axis_size("head")
    rows = gather_z(vector[None])
    rows = jnp.stack(gather_plane(rows))
    rows = jnp.stack([rows, to_other_core(rows)])
    total = 2 * head_count * dp_count
    slot = jnp.arange(total)
    which, plane, step = slot // (head_count * dp_count), (slot // dp_count) % head_count, slot % dp_count
    source = ((ids[0] - step) % dp_count) * 2 * head_count + (ids[1] ^ which) * head_count + (ids[2] ^ plane)
    chosen = (source[None, :] == jnp.arange(total)[:, None]).astype(F32)
    return jnp.dot(chosen, rows.reshape(total, -1), precision=lax.Precision.HIGHEST)


def scatter_small(rows, core, head, dp):
    dp_count, _, head_count = rows.shape[:3]
    half = pick(rows, core, 1) + to_other_core(pick(rows, 1 - core, 1))
    total = pick(half, head, 1)
    for slot in range(1, head_count):
        total = total + to_xor(pick(half, head ^ slot, 1), slot)
    result = pick(total, dp)
    for step in range(1, dp_count):
        result = result + to_shift(pick(total, lax.rem(dp + step, dp_count)), step)
    return result


SLOTS = 4


def causal(block):
    key = lax.broadcasted_iota(jnp.int32, (block, block), 0)
    query = lax.broadcasted_iota(jnp.int32, (block, block), 1)
    return key <= query


def forward_kernel(block, me_ref, qkv, out, lse, scores_a, scores_b):
    me = me_ref[0]
    factor = SCALE * LOG2E
    mask = causal(block)

    def part(which, pos):
        return qkv[(pos % SLOTS) ^ me, which, :, pl.ds((pos // SLOTS) * block, block)]

    for row in range(2 * SLOTS):
        scores = scores_a if row % 2 == 0 else scores_b
        query = part(0, row)
        top = None
        for col in range(row + 1):
            tile = dot(part(1, col), query, 0, 0)
            if col == row:
                tile = jnp.where(mask, tile, -jnp.inf)
            scores[pl.ds(col * block, block), :] = tile
            high = jnp.max(tile, axis=0, keepdims=True)
            top = high if top is None else jnp.maximum(top, high)
        shift = top * factor
        total = jnp.zeros_like(top)
        result = jnp.zeros((HD, block), F32)
        for col in range(row + 1):
            probs = jnp.exp2(scores[pl.ds(col * block, block), :] * factor - shift)
            total = total + jnp.sum(probs, axis=0, keepdims=True)
            result = result + dot(part(2, col), probs.astype(BF16), 1, 0)
        out[(row % SLOTS) ^ me, :, pl.ds((row // SLOTS) * block, block)] = (result / total).astype(BF16)
        lse[pl.ds(row, 1), :] = shift + jnp.log2(total)


def backward_kernel(block, me_ref, qkv, attn, grad_attn, lse, out, grad_q, delta):
    me = me_ref[0]
    factor = SCALE * LOG2E
    mask = causal(block)

    def part(which, pos):
        return qkv[(pos % SLOTS) ^ me, which, :, pl.ds((pos // SLOTS) * block, block)]

    def tokens(ref, pos):
        return ref[(pos % SLOTS) ^ me, :, pl.ds((pos // SLOTS) * block, block)]

    for row in range(2 * SLOTS):
        product = tokens(grad_attn, row).astype(F32) * tokens(attn, row).astype(F32)
        delta[pl.ds(row, 1), :] = jnp.sum(product, axis=0, keepdims=True)
    for col in range(2 * SLOTS):
        key, value = part(1, col), part(2, col)
        grad_key = jnp.zeros((HD, block), F32)
        grad_value = jnp.zeros((HD, block), F32)
        for row in range(col, 2 * SLOTS):
            query, grad_row = part(0, row), tokens(grad_attn, row)
            probs = jnp.exp2(dot(key, query, 0, 0) * factor - lse[pl.ds(row, 1), :])
            if row == col:
                probs = jnp.where(mask, probs, 0.0)
            grad_probs = dot(value, grad_row, 0, 0)
            grad_scores = (probs * (grad_probs - delta[pl.ds(row, 1), :])).astype(BF16)
            grad_value = grad_value + dot(grad_row, probs.astype(BF16), 1, 1)
            grad_key = grad_key + dot(query, grad_scores, 1, 1)
            term = dot(key, grad_scores, 1, 0)
            if col == 0:
                grad_q[row] = term
            else:
                grad_q[row] += term
        where = ((col % SLOTS) ^ me, pl.ds((col // SLOTS) * block, block))
        out[where[0], 1, :, where[1]] = (grad_key * SCALE).astype(BF16)
        out[where[0], 2, :, where[1]] = grad_value.astype(BF16)
    for row in range(2 * SLOTS):
        where = ((row % SLOTS) ^ me, pl.ds((row // SLOTS) * block, block))
        out[where[0], 0, :, where[1]] = (grad_q[row] * SCALE).astype(BF16)


def head_spec(width):
    return pl.BlockSpec((SLOTS, None, HD, width), lambda h, me: (0, h, 0, 0))


def triple_spec(width):
    return pl.BlockSpec((SLOTS, 3, None, HD, width), lambda h, me: (0, 0, h, 0, 0))


def attend(me, qkv):
    heads, width = qkv.shape[2], qkv.shape[4]
    block = width // 2
    length = SLOTS * width
    return pl.pallas_call(
        functools.partial(forward_kernel, block),
        out_shape=(
            jax.ShapeDtypeStruct((SLOTS, heads, HD, width), BF16),
            jax.ShapeDtypeStruct((heads, 2 * SLOTS, block), F32),
        ),
        grid_spec=pltpu.PrefetchScalarGridSpec(
            num_scalar_prefetch=1,
            grid=(heads,),
            in_specs=[triple_spec(width)],
            out_specs=(
                head_spec(width),
                pl.BlockSpec((None, 2 * SLOTS, block), lambda h, me: (h, 0, 0)),
            ),
            scratch_shapes=[pltpu.VMEM((length, block), F32)] * 2,
        ),
        compiler_params=pltpu.CompilerParams(vmem_limit_bytes=VMEM_LIMIT),
        cost_estimate=pl.CostEstimate(
            flops=2 * heads * length * length * HD,
            bytes_accessed=8 * heads * HD * length,
            transcendentals=heads * length * length // 2,
        ),
        name="attend",
    )(me, qkv)


def attend_back(me, qkv, attn, grad_attn, lse):
    heads, width = qkv.shape[2], qkv.shape[4]
    block = width // 2
    length = SLOTS * width
    return pl.pallas_call(
        functools.partial(backward_kernel, block),
        out_shape=jax.ShapeDtypeStruct(qkv.shape, BF16),
        grid_spec=pltpu.PrefetchScalarGridSpec(
            num_scalar_prefetch=1,
            grid=(heads,),
            in_specs=[
                triple_spec(width),
                head_spec(width),
                head_spec(width),
                pl.BlockSpec((None, 2 * SLOTS, block), lambda h, me: (h, 0, 0)),
            ],
            out_specs=triple_spec(width),
            scratch_shapes=[
                pltpu.VMEM((2 * SLOTS, HD, block), F32),
                pltpu.VMEM((2 * SLOTS, block), F32),
            ],
        ),
        compiler_params=pltpu.CompilerParams(vmem_limit_bytes=VMEM_LIMIT),
        cost_estimate=pl.CostEstimate(
            flops=5 * heads * length * length * HD,
            bytes_accessed=16 * heads * HD * length,
            transcendentals=heads * length * length // 2,
        ),
        name="attend_back",
    )(me, qkv, attn, grad_attn, lse)


def feed_kernel(ctx, weight, bias, hidden, slope):
    pre = dot(ctx[...], weight[...], 1, 0) + bias[...]
    value, steep = gelu_pair(pre)
    hidden[...] = value.astype(BF16)
    slope[...] = steep


def feed(ctx, weight, bias):
    rows, width = ctx.shape
    units = weight.shape[1]
    block = min(512, units)
    return pl.pallas_call(
        feed_kernel,
        out_shape=(
            jax.ShapeDtypeStruct((rows, units), BF16),
            jax.ShapeDtypeStruct((rows, units), F32),
        ),
        grid=(units // block,),
        in_specs=[
            pl.BlockSpec((rows, width), lambda i: (0, 0)),
            pl.BlockSpec((width, block), lambda i: (0, i)),
            pl.BlockSpec((1, block), lambda i: (0, i)),
        ],
        out_specs=(
            pl.BlockSpec((rows, block), lambda i: (0, i)),
            pl.BlockSpec((rows, block), lambda i: (0, i)),
        ),
        compiler_params=pltpu.CompilerParams(vmem_limit_bytes=VMEM_LIMIT),
        cost_estimate=pl.CostEstimate(
            flops=2 * rows * width * units,
            bytes_accessed=2 * width * units + 6 * rows * units,
            transcendentals=rows * units,
        ),
        name="feed",
    )(ctx, weight, bias.reshape(1, -1))


def feed_back_kernel(
    cot, hidden, slope, w_fc, w_proj, base, pre_low, grad_bias, grad_ctx, stream, sum_ctx, sum_out
):
    step = pl.program_id(0)
    grad_pre = dot(cot[...], w_proj[...], 1, 1) * slope[...]
    grad_bias[...] = jnp.sum(grad_pre, axis=0, keepdims=True)
    low = grad_pre.astype(BF16)
    pre_low[...] = low
    back = dot(low, w_fc[...], 1, 1)
    ahead = dot(hidden[...], w_proj[...], 1, 0)

    @pl.when(step == 0)
    def _():
        sum_ctx[...] = back
        sum_out[...] = base[...] + ahead

    @pl.when(step > 0)
    def _():
        sum_ctx[...] += back
        sum_out[...] += ahead

    @pl.when(step == pl.num_programs(0) - 1)
    def _():
        grad_ctx[...] = sum_ctx[...]
        stream[...] = sum_out[...]


def feed_back(cot, hidden, slope, w_fc, w_proj, base):
    rows, width = cot.shape
    units = hidden.shape[1]
    block = min(512, units)
    whole = pl.BlockSpec((rows, width), lambda i: (0, 0))
    columns = pl.BlockSpec((rows, block), lambda i: (0, i))
    return pl.pallas_call(
        feed_back_kernel,
        out_shape=(
            jax.ShapeDtypeStruct((rows, units), BF16),
            jax.ShapeDtypeStruct((1, units), F32),
            jax.ShapeDtypeStruct((rows, width), F32),
            jax.ShapeDtypeStruct((rows, width), F32),
        ),
        grid=(units // block,),
        in_specs=[
            whole,
            columns,
            columns,
            pl.BlockSpec((width, block), lambda i: (0, i)),
            pl.BlockSpec((block, width), lambda i: (i, 0)),
            whole,
        ],
        out_specs=(columns, pl.BlockSpec((1, block), lambda i: (0, i)), whole, whole),
        scratch_shapes=[pltpu.VMEM((rows, width), F32)] * 2,
        compiler_params=pltpu.CompilerParams(vmem_limit_bytes=VMEM_LIMIT),
        cost_estimate=pl.CostEstimate(
            flops=6 * rows * width * units,
            bytes_accessed=4 * width * units + 8 * rows * units,
            transcendentals=0,
        ),
        name="feed_back",
    )(cot, hidden, slope, w_fc, w_proj, base)


def split_rows(core, value, own, away):
    count, rows = own.shape[0], own.shape[2]
    value = value.astype(BF16)
    half = count * rows
    first = value[:half].reshape(count, 1, rows, -1)
    second = value[half:].reshape(count, 1, rows, -1)

    @pl.when(core == 0)
    def _():
        own[...] = first
        away[...] = second

    @pl.when(core == 1)
    def _():
        own[...] = second
        away[...] = first


def weight_kernel(ids, left, right, own, away):
    split_rows(ids[1], dot(left[...], right[...], 0, 0), own, away)


def weight_pair_kernel(ids, left, right, attn, resid, own, away):
    units = right.shape[1]
    total = dot(attn[0], resid[0], 1, 0)
    for seq in range(1, attn.shape[0]):
        total = total + dot(attn[seq], resid[seq], 1, 0)
    split_rows(ids[1], dot(left[...], right[...], 0, 0), own.at[..., pl.ds(0, units)], away.at[..., pl.ds(0, units)])
    split_rows(ids[1], total, own.at[..., pl.ds(units, total.shape[1])], away.at[..., pl.ds(units, total.shape[1])])


def weight_call(kernel, counts, rows, columns, in_specs, flops, name):
    dp_count, head_count = counts
    spec = pl.BlockSpec((head_count, 1, rows, columns), lambda d, ids: (0, d, 0, 0))
    shape = jax.ShapeDtypeStruct((head_count, dp_count, rows, columns), BF16)
    return pl.pallas_call(
        kernel,
        out_shape=(shape, shape),
        grid_spec=pltpu.PrefetchScalarGridSpec(
            num_scalar_prefetch=1, grid=(dp_count,), in_specs=in_specs, out_specs=(spec, spec)
        ),
        compiler_params=pltpu.CompilerParams(vmem_limit_bytes=VMEM_LIMIT),
        cost_estimate=pl.CostEstimate(
            flops=flops, bytes_accessed=4 * head_count * dp_count * rows * columns, transcendentals=0
        ),
        name=name,
    )


def weight_terms(ids, left, right, counts, rows):
    tokens, columns = right.shape
    span = 2 * counts[1] * rows
    return weight_call(
        weight_kernel,
        counts,
        rows,
        columns,
        [
            pl.BlockSpec((tokens, span), lambda d, ids: (0, d)),
            pl.BlockSpec((tokens, columns), lambda d, ids: (0, 0)),
        ],
        2 * tokens * columns * left.shape[1],
        "weight_terms",
    )(ids, left, right)


def weight_pair_terms(ids, left, right, attn, resid, counts, rows):
    tokens, units = right.shape
    seqs, _, features, seq_tokens = attn.shape
    width = resid.shape[2]
    span = 2 * counts[1] * rows
    return weight_call(
        weight_pair_kernel,
        counts,
        rows,
        units + width,
        [
            pl.BlockSpec((tokens, span), lambda d, ids: (0, d)),
            pl.BlockSpec((tokens, units), lambda d, ids: (0, 0)),
            pl.BlockSpec((seqs, None, features, seq_tokens), lambda d, ids: (0, d ^ ids[2], 0, 0)),
            pl.BlockSpec(resid.shape, lambda d, ids: (0, 0, 0)),
        ],
        2 * tokens * (units + width) * left.shape[1],
        "weight_pair_terms",
    )(ids, left, right, attn, resid)


def to_attention(slots, head):
    count, features, width = slots.shape
    if count == SLOTS:
        return head.reshape(1), slots
    order = jnp.arange(count) ^ head
    natural = slots[order].reshape(count, features, 2, width // 2)
    tokens = natural.transpose(1, 2, 0, 3).reshape(features, 2, SLOTS, -1)
    return jnp.zeros((1,), jnp.int32), tokens.transpose(2, 0, 1, 3).reshape(SLOTS, features, -1)


def from_attention(tokens, head, count):
    if count == SLOTS:
        return tokens
    features = tokens.shape[1]
    natural = tokens.reshape(SLOTS, features, 2, -1).transpose(1, 2, 0, 3)
    natural = natural.reshape(features, 2, count, -1).transpose(2, 0, 1, 3)
    return natural.reshape(count, features, -1)[jnp.arange(count) ^ head]


def on_device(
    stream_in,
    ln1_gain,
    ln1_bias,
    w_qkv,
    b_qv,
    w_out,
    b_out,
    ln2_gain,
    ln2_bias,
    w_fc,
    b_fc,
    w_proj,
    b_proj,
    cotangent,
):
    seq_dev, tok_rows, width = stream_in.shape
    rows = seq_dev * tok_rows
    dp_count, head_count = lax.axis_size("dp"), lax.axis_size("head")
    devices = dp_count * 2 * head_count
    grid = (dp_count, 2, head_count)
    dp, core, head = lax.axis_index("dp"), lax.axis_index("blk"), lax.axis_index("head")
    ids = jnp.stack([dp, core, head]).astype(jnp.int32)
    group = width // head_count
    heads = group // HD
    own_rows = w_qkv.shape[0]
    hidden_width = w_fc.shape[1]

    sizes = [own_rows] * 8 + [b_fc.shape[0]]
    small = jnp.concatenate(
        [ln1_gain, ln1_bias, b_qv[0], b_qv[1], b_out, ln2_gain, ln2_bias, b_proj, b_fc]
    ).astype(F32)
    small = gather_small(small, ids)
    edges = [sum(sizes[:i]) for i in range(len(sizes) + 1)]
    full = [small[:, edges[i] : edges[i + 1]].reshape(-1) for i in range(len(sizes))]
    gain_one, bias_one, bias_q, bias_v, bias_out, gain_two, bias_two, bias_proj, bias_fc = full

    square = head_count == 4
    stream_rows = stream_in.reshape(rows, width)
    normed_one, inv_one = normalize(stream_rows)
    act_one = (normed_one * gain_one + bias_one).astype(BF16).reshape(seq_dev, tok_rows, width)

    columns = w_qkv.reshape(own_rows, 3, head_count, group)
    parts = [
        pick(columns, head ^ slot, 2).reshape(own_rows, 3 * group) for slot in range(head_count)
    ]
    parts = [parts[0]] + [to_xor(parts[slot], slot) for slot in range(1, head_count)]
    one_z = gather_dp(jnp.concatenate([w_fc, w_out], axis=1))
    two_z = gather_dp(w_proj)

    own_half = by_half(core, pick(act_one, core), to_other_core(pick(act_one, 1 - core)))
    own_half = own_half.reshape(2 * tok_rows, width)
    own_half, shard = together(own_half, jnp.concatenate(parts, axis=1))
    group_z = gather_z(shard)
    group_z = jnp.stack([pick(group_z, (dp + dp_count - k) % dp_count) for k in range(dp_count)])
    wide = 3 * group
    (group_w,) = place(
        [group_z[:, :, slot * wide : (slot + 1) * wide] for slot in range(head_count)],
        (wide,),
        ids,
    )
    acts = plane_far(own_half, plane_near(own_half), 0) if square else gather_plane(own_half)
    *acts, one_z = together(*acts, one_z)
    one_near = plane_near(one_z) if square else gather_plane(one_z)
    qkv_bias = jnp.concatenate(
        [
            pick(bias_q.reshape(head_count, group), head),
            jnp.zeros((group,), F32),
            pick(bias_v.reshape(head_count, group), head),
        ]
    )[:, None]
    qkv_slots = jnp.stack([(dot(group_w, act, 0, 1) + qkv_bias).astype(BF16) for act in acts])
    me, qkv = to_attention(qkv_slots, head)
    qkv = qkv.reshape(SLOTS, 3, heads, HD, -1)
    attn, lse = attend(me, qkv)
    attn, two_z, *one_near = together(attn, two_z, *one_near)
    attn_slots = from_attention(attn.reshape(SLOTS, group, -1), head, head_count)
    attn_all = [attn_slots[0]] + [to_xor(attn_slots[j], j) for j in range(1, head_count)]
    one_pieces = plane_far(one_z, one_near, 2) if square else one_near
    attn_all = jnp.stack(attn_all)
    first, second = attn_all[:, :, :tok_rows], attn_all[:, :, tok_rows:]
    keep = jnp.where(core == 0, first, second)
    away = jnp.where(core == 0, second, first)
    attn_cols = by_half(core, keep, to_other_core(away))

    attn_cols, two_z, *one_pieces = together(attn_cols, two_z, *one_pieces)
    two_near = plane_near(two_z) if square else gather_plane(two_z)
    full_wfc, full_wout = place(one_pieces, (hidden_width, width), ids)
    slot_wout = full_wout.reshape(head_count, group, width)
    slot_wout = jnp.stack([pick(slot_wout, head ^ slot) for slot in range(head_count)])

    resid = (
        stream_rows
        + jnp.einsum("sjdt,jde->ste", attn_cols, slot_wout, preferred_element_type=F32).reshape(
            rows, width
        )
        + bias_out
    )
    normed_two, inv_two = normalize(resid)
    ctx = (normed_two * gain_two + bias_two).astype(BF16)
    ctx, *two_near = together(ctx, *two_near)
    two_pieces = plane_far(two_z, two_near, 1) if square else two_near
    hidden, slope = feed(ctx, full_wfc, bias_fc)
    hidden, *two_pieces = together(hidden, *two_pieces)
    cot_rows = cotangent.reshape(rows, width)
    cot_low = cot_rows.astype(BF16)
    grad_b_proj = jnp.sum(cot_rows, axis=0)
    chips = (dp_count, head_count)
    aligned = group == 2 * head_count * own_rows and (head_count * own_rows) % 128 == 0
    if aligned:
        two_own, two_away = weight_terms(ids, hidden, cot_low, chips, w_proj.shape[0])
    else:
        two_own, two_away = split_terms(
            dot(hidden, cot_low, 0, 0).astype(BF16).reshape(grid + (-1, width)), core
        )
    two_terms = chip_terms(two_own, two_away)
    (full_wproj,) = place(two_pieces, (width,), ids)
    two_terms, cot_low = together(two_terms, cot_low)
    two_plane = scatter_plane(two_terms)
    pre_low, grad_b_fc, grad_ctx, stream_out = feed_back(
        cot_low, hidden, slope, full_wfc, full_wproj, resid + bias_proj
    )
    grad_b_fc = grad_b_fc.reshape(-1)
    grad_ln2_gain = jnp.sum(grad_ctx * normed_two, axis=0)
    grad_ln2_bias = jnp.sum(grad_ctx, axis=0)
    grad_resid = cot_rows + norm_back(grad_ctx * gain_two, normed_two, inv_two)
    grad_b_out = jnp.sum(grad_resid, axis=0)
    resid_low = grad_resid.astype(BF16)
    resid_three = resid_low.reshape(seq_dev, tok_rows, width)
    grad_attn_cols = jnp.einsum(
        "ste,jde->sjdt", resid_three, slot_wout, preferred_element_type=F32
    ).astype(BF16)
    kept = pick(grad_attn_cols, core)
    arrived = to_other_core(pick(grad_attn_cols, 1 - core))
    grad_half = jnp.where(
        core == 0,
        jnp.concatenate([kept, arrived], axis=2),
        jnp.concatenate([arrived, kept], axis=2),
    )
    grad_half, two_plane = together(grad_half, two_plane)
    shard_wproj = scatter_dp(two_plane)
    grad_slots = [grad_half[0]] + [to_xor(grad_half[j], j) for j in range(1, head_count)]

    if aligned:
        one_own, one_away = weight_pair_terms(
            ids, ctx, pre_low, attn_cols, resid_three, chips, own_rows
        )
    else:
        grad_w_fc = dot(ctx, pre_low, 0, 0).astype(BF16)
        grad_w_out = jnp.einsum(
            "sjdt,ste->jde", attn_cols, resid_three, preferred_element_type=F32
        ).astype(BF16)
        grad_w_out = jnp.stack([pick(grad_w_out, head ^ slot) for slot in range(head_count)])
        one_own, one_away = split_terms(
            jnp.concatenate(
                [
                    grad_w_fc.reshape(grid + (-1, hidden_width)),
                    grad_w_out.reshape(grid + (-1, width)),
                ],
                axis=4,
            ),
            core,
        )
    one_terms = chip_terms(one_own, one_away)
    *grad_slots, one_terms = together(*grad_slots, one_terms)
    one_plane = scatter_plane(one_terms)

    _, grad_attn = to_attention(jnp.stack(grad_slots), head)
    grad_attn = grad_attn.reshape(SLOTS, heads, HD, -1)
    grad_qkv = attend_back(me, qkv, attn, grad_attn, lse)
    grad_qkv = from_attention(grad_qkv.reshape(SLOTS, 3 * group, -1), head, head_count)

    act_parts = [dot(grad_qkv[slot], group_w, 0, 1) for slot in range(head_count)]
    act_parts = [act_parts[0]] + [part.astype(BF16) for part in act_parts[1:]]
    act_terms = [to_xor(act_parts[j], j) for j in range(1, head_count)]
    grad_group_w = dot(acts[0], grad_qkv[0], 0, 1)
    for slot in range(1, head_count):
        grad_group_w = grad_group_w + dot(acts[slot], grad_qkv[slot], 0, 1)
    token_sums = jnp.sum(grad_qkv.astype(F32), axis=(0, 2)).reshape(3, group)
    grad_bias = jnp.zeros((3, head_count, group), F32)
    grad_bias = lax.dynamic_update_index_in_dim(grad_bias, token_sums, head, 1).reshape(3, width)

    wide_w = group_w.astype(F32)
    act_sum = jnp.sum(wide_w * token_sums.reshape(1, -1), axis=1)
    act_product = jnp.sum(wide_w * grad_group_w, axis=1)
    vectors = [
        act_product,
        act_sum,
        grad_bias[0],
        grad_bias[2],
        grad_b_out,
        grad_ln2_gain,
        grad_ln2_bias,
        grad_b_proj,
        grad_b_fc,
    ]
    packed = jnp.concatenate([v.reshape(devices, -1) for v in vectors], axis=1)
    mine = scatter_small(packed.reshape(grid + (-1,)), core, head, dp)
    grad_group_w = grad_group_w.astype(BF16).reshape(grid + (own_rows, 3 * group))
    half_w = pick(grad_group_w, core, 1).astype(F32) + core_terms(grad_group_w, core).astype(F32)
    shard_w = scatter_z(half_w, dp)
    act_terms[0], one_plane, mine = together(act_terms[0], one_plane, mine)
    shard_w, shard_one, *act_terms = together(shard_w, scatter_dp(one_plane), *act_terms)
    sums = plane_total(act_parts[0], act_terms).reshape(2, tok_rows, width)
    grad_act = by_half(
        core, pick(sums, core), to_other_core(pick(sums, 1 - core))
    ).reshape(rows, width)

    pieces = jnp.stack(
        [pick(shard_w, head)]
        + [to_xor(pick(shard_w, head ^ slot), slot) for slot in range(1, head_count)]
    )
    ordered = [pick(pieces, head ^ slot) for slot in range(head_count)]
    shard_wqkv = jnp.concatenate(
        [piece[:, c * group : (c + 1) * group] for c in range(3) for piece in ordered], axis=1
    )

    shard_wfc, shard_wout = shard_one[:, :hidden_width], shard_one[:, hidden_width:]
    grad_rows_in = grad_resid + norm_back(grad_act * gain_one, normed_one, inv_one)

    cut = [mine[edges[i] : edges[i + 1]] for i in range(len(sizes))]
    return (
        stream_out.reshape(seq_dev, tok_rows, width),
        grad_rows_in.reshape(seq_dev, tok_rows, width),
        (cut[0] - ln1_bias.astype(F32) * cut[1]) / ln1_gain.astype(F32),
        cut[1],
        shard_wqkv,
        jnp.stack([cut[2], cut[3]]),
        shard_wout.reshape(-1, width),
        cut[4],
        cut[5],
        cut[6],
        shard_wfc.reshape(-1, hidden_width),
        cut[8],
        shard_wproj.reshape(-1, width),
        cut[7],
    )


def solution(mesh):
    every = ("dp", "blk", "head")
    tokens = P("dp", ("blk", "head"), None)
    vector, matrix = P(every), P(every, None)
    in_specs = (
        tokens,
        vector,
        vector,
        matrix,
        P(None, every),
        matrix,
        vector,
        vector,
        vector,
        matrix,
        vector,
        matrix,
        vector,
        tokens,
    )
    out_specs = (
        tokens,
        tokens,
        vector,
        vector,
        matrix,
        P(None, every),
        matrix,
        vector,
        vector,
        vector,
        matrix,
        vector,
        matrix,
        vector,
    )
    return jax.shard_map(
        on_device, mesh=mesh, in_specs=in_specs, out_specs=out_specs, check_vma=False
    )
```

```python
import functools
import math

import jax
import jax.numpy as jnp
from jax import lax
from jax.experimental import pallas as pl
from jax.experimental.pallas import tpu as pltpu
from jax.sharding import PartitionSpec as P

HD = 64
EPSILON = 1e-05
GELU_COEF = 0.044715
ROOT_TWO_PI = math.sqrt(2.0 / math.pi)
SCALE = 1.0 / math.sqrt(HD)
LOG2E = math.log2(math.e)
F32 = jnp.float32
BF16 = jnp.bfloat16
VMEM_LIMIT = 48 * 1024 * 1024


def normalize(stream):
    centred = stream - jnp.mean(stream, axis=-1, keepdims=True)
    inv_std = lax.rsqrt(jnp.mean(centred * centred, axis=-1, keepdims=True) + EPSILON)
    return (centred * inv_std, inv_std)


def norm_back(grad_normed, normed, inv_std):
    return inv_std * (
        grad_normed
        - jnp.mean(grad_normed, axis=-1, keepdims=True)
        - normed * jnp.mean(grad_normed * normed, axis=-1, keepdims=True)
    )


def gelu_pair(pre_act):
    square = pre_act * pre_act
    upper = 0.5 + 0.5 * jnp.tanh(pre_act * (ROOT_TWO_PI + (ROOT_TWO_PI * GELU_COEF) * square))
    bend = 2.0 * ROOT_TWO_PI + (6.0 * ROOT_TWO_PI * GELU_COEF) * square
    return (pre_act * upper, upper + upper * (pre_act * (1.0 - upper)) * bend)


def dot(left, right, left_dim, right_dim):
    return lax.dot_general(
        left, right, (((left_dim,), (right_dim,)), ((), ())), preferred_element_type=F32
    )


def to_xor(value, step):
    count = lax.axis_size("head")
    return lax.ppermute(value, "head", [(i, i ^ step) for i in range(count)])


def to_shift(value, step):
    count = lax.axis_size("dp")
    return lax.ppermute(value, "dp", [(i, (i + step) % count) for i in range(count)])


def to_other_core(value):
    return lax.ppermute(value, "blk", [(0, 1), (1, 0)])


def pick(stacked, index, axis=0):
    return lax.dynamic_index_in_dim(stacked, index, axis, keepdims=False)


def by_half(core, own, other):
    return jnp.where(core == 0, jnp.stack([own, other]), jnp.stack([other, own]))


def place_kernel(widths, ids, *refs):
    count = (len(refs) - 1 - len(widths)) // 2
    pieces, outs, sem = refs[: 2 * count], refs[2 * count : -1], refs[-1]
    core, head = ids[1], ids[2]
    copies = []
    for which in range(2):
        for slot in range(count):
            start = 0
            for out, columns in zip(outs, widths):
                copies.append(
                    pltpu.make_async_copy(
                        pieces[which * count + slot].at[:, :, pl.ds(start, columns)],
                        out.at[:, core ^ which, head ^ slot],
                        sem.at[len(copies)],
                    )
                )
                start += columns
    for copy in copies:
        copy.start()
    for copy in copies:
        copy.wait()


def place(mine, widths, ids):
    dp_count, rows, _ = mine[0].shape
    pieces = list(mine) + [to_other_core(piece) for piece in mine]
    shapes = [(dp_count, 2, len(mine), rows, columns) for columns in widths]
    outs = pl.pallas_call(
        functools.partial(place_kernel, widths),
        out_shape=[jax.ShapeDtypeStruct(shape, BF16) for shape in shapes],
        grid_spec=pltpu.PrefetchScalarGridSpec(
            num_scalar_prefetch=1,
            grid=(1,),
            in_specs=[pl.BlockSpec(memory_space=pl.ANY)] * len(pieces),
            out_specs=[
                pl.BlockSpec(
                    shape, lambda i, ids: (0, 0, 0, 0, 0), pipeline_mode=pl.Buffered(1)
                )
                for shape in shapes
            ],
            scratch_shapes=[pltpu.SemaphoreType.DMA((len(pieces) * len(widths),))],
        ),
        compiler_params=pltpu.CompilerParams(vmem_limit_bytes=VMEM_LIMIT),
        name="place",
    )(ids, *pieces)
    return [out.reshape(-1, columns) for out, columns in zip(outs, widths)]


def gather_dp(shard):
    full = lax.all_gather(shard, "dp", axis=0, tiled=True)
    return full.reshape((-1,) + shard.shape)


def split_terms(grad, core):
    return (
        pick(grad, core, 1).transpose(1, 0, 2, 3),
        pick(grad, 1 - core, 1).transpose(1, 0, 2, 3),
    )


def chip_terms(own, away):
    total = (own.astype(F32) + to_other_core(away).astype(F32)).astype(BF16)
    return total.reshape(-1, total.shape[-1])


def scatter_plane(terms):
    return lax.psum_scatter(terms, "head", scatter_dimension=0, tiled=True)


def scatter_dp(terms):
    return lax.psum_scatter(terms, "dp", scatter_dimension=0, tiled=True).astype(F32)


def gather_z(shard):
    return jnp.stack([shard] + [to_shift(shard, k) for k in range(1, lax.axis_size("dp"))])


def gather_plane(own):
    return [own] + [to_xor(own, j) for j in range(1, lax.axis_size("head"))]


def plane_near(own):
    return to_xor(own, 1), to_xor(own, 2)


def plane_far(own, near, axis):
    half = own.shape[axis] // 2
    lower = to_xor(lax.slice_in_dim(near[0], 0, half, axis=axis), 2)
    upper = to_xor(lax.slice_in_dim(near[1], half, 2 * half, axis=axis), 1)
    return [own, near[0], near[1], jnp.concatenate([lower, upper], axis=axis)]


def core_terms(grad, core):
    return to_other_core(pick(grad, 1 - core, 1))


def plane_total(own, terms):
    total = own
    for piece in terms:
        total = total + piece.astype(F32)
    return total


def scatter_z(total, dp):
    dp_count = total.shape[0]
    low = total.astype(BF16)
    result = pick(total, dp)
    for step in range(1, dp_count):
        result = result + to_shift(pick(low, lax.rem(dp + step, dp_count)), step).astype(F32)
    return result


def together(*values):
    return lax.optimization_barrier(values)


def gather_small(vector, ids):
    dp_count, head_count = lax.axis_size("dp"), lax.axis_size("head")
    rows = gather_z(vector[None])
    rows = jnp.stack(gather_plane(rows))
    rows = jnp.stack([rows, to_other_core(rows)])
    total = 2 * head_count * dp_count
    slot = jnp.arange(total)
    which, plane, step = slot // (head_count * dp_count), (slot // dp_count) % head_count, slot % dp_count
    source = ((ids[0] - step) % dp_count) * 2 * head_count + (ids[1] ^ which) * head_count + (ids[2] ^ plane)
    chosen = (source[None, :] == jnp.arange(total)[:, None]).astype(F32)
    return jnp.dot(chosen, rows.reshape(total, -1), precision=lax.Precision.HIGHEST)


def scatter_small(rows, core, head, dp):
    dp_count, _, head_count = rows.shape[:3]
    half = pick(rows, core, 1) + to_other_core(pick(rows, 1 - core, 1))
    total = pick(half, head, 1)
    for slot in range(1, head_count):
        total = total + to_xor(pick(half, head ^ slot, 1), slot)
    result = pick(total, dp)
    for step in range(1, dp_count):
        result = result + to_shift(pick(total, lax.rem(dp + step, dp_count)), step)
    return result


SLOTS = 4


def causal(block):
    key = lax.broadcasted_iota(jnp.int32, (block, block), 0)
    query = lax.broadcasted_iota(jnp.int32, (block, block), 1)
    return key <= query


def forward_kernel(block, me_ref, qkv, out, lse, scores_a, scores_b):
    me = me_ref[0]
    factor = SCALE * LOG2E
    mask = causal(block)

    def part(which, pos):
        return qkv[(pos % SLOTS) ^ me, which, :, pl.ds((pos // SLOTS) * block, block)]

    for row in range(2 * SLOTS):
        scores = scores_a if row % 2 == 0 else scores_b
        query = part(0, row)
        top = None
        for col in range(row + 1):
            tile = dot(part(1, col), query, 0, 0)
            if col == row:
                tile = jnp.where(mask, tile, -jnp.inf)
            scores[pl.ds(col * block, block), :] = tile
            high = jnp.max(tile, axis=0, keepdims=True)
            top = high if top is None else jnp.maximum(top, high)
        shift = top * factor
        total = jnp.zeros_like(top)
        result = jnp.zeros((HD, block), F32)
        for col in range(row + 1):
            probs = jnp.exp2(scores[pl.ds(col * block, block), :] * factor - shift)
            total = total + jnp.sum(probs, axis=0, keepdims=True)
            result = result + dot(part(2, col), probs.astype(BF16), 1, 0)
        out[(row % SLOTS) ^ me, :, pl.ds((row // SLOTS) * block, block)] = (result / total).astype(BF16)
        lse[pl.ds(row, 1), :] = shift + jnp.log2(total)


def backward_kernel(block, me_ref, qkv, attn, grad_attn, lse, out, grad_q, delta):
    me = me_ref[0]
    factor = SCALE * LOG2E
    mask = causal(block)

    def part(which, pos):
        return qkv[(pos % SLOTS) ^ me, which, :, pl.ds((pos // SLOTS) * block, block)]

    def tokens(ref, pos):
        return ref[(pos % SLOTS) ^ me, :, pl.ds((pos // SLOTS) * block, block)]

    for row in range(2 * SLOTS):
        product = tokens(grad_attn, row).astype(F32) * tokens(attn, row).astype(F32)
        delta[pl.ds(row, 1), :] = jnp.sum(product, axis=0, keepdims=True)
    for col in range(2 * SLOTS):
        key, value = part(1, col), part(2, col)
        grad_key = jnp.zeros((HD, block), F32)
        grad_value = jnp.zeros((HD, block), F32)
        for row in range(col, 2 * SLOTS):
            query, grad_row = part(0, row), tokens(grad_attn, row)
            probs = jnp.exp2(dot(key, query, 0, 0) * factor - lse[pl.ds(row, 1), :])
            if row == col:
                probs = jnp.where(mask, probs, 0.0)
            grad_probs = dot(value, grad_row, 0, 0)
            grad_scores = (probs * (grad_probs - delta[pl.ds(row, 1), :])).astype(BF16)
            grad_value = grad_value + dot(grad_row, probs.astype(BF16), 1, 1)
            grad_key = grad_key + dot(query, grad_scores, 1, 1)
            term = dot(key, grad_scores, 1, 0)
            if col == 0:
                grad_q[row] = term
            else:
                grad_q[row] += term
        where = ((col % SLOTS) ^ me, pl.ds((col // SLOTS) * block, block))
        out[where[0], 1, :, where[1]] = (grad_key * SCALE).astype(BF16)
        out[where[0], 2, :, where[1]] = grad_value.astype(BF16)
    for row in range(2 * SLOTS):
        where = ((row % SLOTS) ^ me, pl.ds((row // SLOTS) * block, block))
        out[where[0], 0, :, where[1]] = (grad_q[row] * SCALE).astype(BF16)


def head_spec(width):
    return pl.BlockSpec((SLOTS, None, HD, width), lambda h, me: (0, h, 0, 0))


def triple_spec(width):
    return pl.BlockSpec((SLOTS, 3, None, HD, width), lambda h, me: (0, 0, h, 0, 0))


def attend(me, qkv):
    heads, width = qkv.shape[2], qkv.shape[4]
    block = width // 2
    length = SLOTS * width
    return pl.pallas_call(
        functools.partial(forward_kernel, block),
        out_shape=(
            jax.ShapeDtypeStruct((SLOTS, heads, HD, width), BF16),
            jax.ShapeDtypeStruct((heads, 2 * SLOTS, block), F32),
        ),
        grid_spec=pltpu.PrefetchScalarGridSpec(
            num_scalar_prefetch=1,
            grid=(heads,),
            in_specs=[triple_spec(width)],
            out_specs=(
                head_spec(width),
                pl.BlockSpec((None, 2 * SLOTS, block), lambda h, me: (h, 0, 0)),
            ),
            scratch_shapes=[pltpu.VMEM((length, block), F32)] * 2,
        ),
        compiler_params=pltpu.CompilerParams(vmem_limit_bytes=VMEM_LIMIT),
        cost_estimate=pl.CostEstimate(
            flops=2 * heads * length * length * HD,
            bytes_accessed=8 * heads * HD * length,
            transcendentals=heads * length * length // 2,
        ),
        name="attend",
    )(me, qkv)


def attend_back(me, qkv, attn, grad_attn, lse):
    heads, width = qkv.shape[2], qkv.shape[4]
    block = width // 2
    length = SLOTS * width
    return pl.pallas_call(
        functools.partial(backward_kernel, block),
        out_shape=jax.ShapeDtypeStruct(qkv.shape, BF16),
        grid_spec=pltpu.PrefetchScalarGridSpec(
            num_scalar_prefetch=1,
            grid=(heads,),
            in_specs=[
                triple_spec(width),
                head_spec(width),
                head_spec(width),
                pl.BlockSpec((None, 2 * SLOTS, block), lambda h, me: (h, 0, 0)),
            ],
            out_specs=triple_spec(width),
            scratch_shapes=[
                pltpu.VMEM((2 * SLOTS, HD, block), F32),
                pltpu.VMEM((2 * SLOTS, block), F32),
            ],
        ),
        compiler_params=pltpu.CompilerParams(vmem_limit_bytes=VMEM_LIMIT),
        cost_estimate=pl.CostEstimate(
            flops=5 * heads * length * length * HD,
            bytes_accessed=16 * heads * HD * length,
            transcendentals=heads * length * length // 2,
        ),
        name="attend_back",
    )(me, qkv, attn, grad_attn, lse)


def feed_kernel(ctx, weight, bias, hidden, slope):
    pre = dot(ctx[...], weight[...], 1, 0) + bias[...]
    value, steep = gelu_pair(pre)
    hidden[...] = value.astype(BF16)
    slope[...] = steep


def feed(ctx, weight, bias):
    rows, width = ctx.shape
    units = weight.shape[1]
    block = min(512, units)
    return pl.pallas_call(
        feed_kernel,
        out_shape=(
            jax.ShapeDtypeStruct((rows, units), BF16),
            jax.ShapeDtypeStruct((rows, units), F32),
        ),
        grid=(units // block,),
        in_specs=[
            pl.BlockSpec((rows, width), lambda i: (0, 0)),
            pl.BlockSpec((width, block), lambda i: (0, i)),
            pl.BlockSpec((1, block), lambda i: (0, i)),
        ],
        out_specs=(
            pl.BlockSpec((rows, block), lambda i: (0, i)),
            pl.BlockSpec((rows, block), lambda i: (0, i)),
        ),
        compiler_params=pltpu.CompilerParams(vmem_limit_bytes=VMEM_LIMIT),
        cost_estimate=pl.CostEstimate(
            flops=2 * rows * width * units,
            bytes_accessed=2 * width * units + 6 * rows * units,
            transcendentals=rows * units,
        ),
        name="feed",
    )(ctx, weight, bias.reshape(1, -1))


def feed_back_kernel(
    cot, hidden, slope, w_fc, w_proj, base, pre_low, grad_bias, grad_ctx, stream, sum_ctx, sum_out
):
    step = pl.program_id(0)
    grad_pre = dot(cot[...], w_proj[...], 1, 1) * slope[...]
    grad_bias[...] = jnp.sum(grad_pre, axis=0, keepdims=True)
    low = grad_pre.astype(BF16)
    pre_low[...] = low
    back = dot(low, w_fc[...], 1, 1)
    ahead = dot(hidden[...], w_proj[...], 1, 0)

    @pl.when(step == 0)
    def _():
        sum_ctx[...] = back
        sum_out[...] = base[...] + ahead

    @pl.when(step > 0)
    def _():
        sum_ctx[...] += back
        sum_out[...] += ahead

    @pl.when(step == pl.num_programs(0) - 1)
    def _():
        grad_ctx[...] = sum_ctx[...]
        stream[...] = sum_out[...]


def feed_back(cot, hidden, slope, w_fc, w_proj, base):
    rows, width = cot.shape
    units = hidden.shape[1]
    block = min(1024, units)
    whole = pl.BlockSpec((rows, width), lambda i: (0, 0))
    columns = pl.BlockSpec((rows, block), lambda i: (0, i))
    return pl.pallas_call(
        feed_back_kernel,
        out_shape=(
            jax.ShapeDtypeStruct((rows, units), BF16),
            jax.ShapeDtypeStruct((1, units), F32),
            jax.ShapeDtypeStruct((rows, width), F32),
            jax.ShapeDtypeStruct((rows, width), F32),
        ),
        grid=(units // block,),
        in_specs=[
            whole,
            columns,
            columns,
            pl.BlockSpec((width, block), lambda i: (0, i)),
            pl.BlockSpec((block, width), lambda i: (i, 0)),
            whole,
        ],
        out_specs=(columns, pl.BlockSpec((1, block), lambda i: (0, i)), whole, whole),
        scratch_shapes=[pltpu.VMEM((rows, width), F32)] * 2,
        compiler_params=pltpu.CompilerParams(vmem_limit_bytes=VMEM_LIMIT),
        cost_estimate=pl.CostEstimate(
            flops=6 * rows * width * units,
            bytes_accessed=4 * width * units + 8 * rows * units,
            transcendentals=0,
        ),
        name="feed_back",
    )(cot, hidden, slope, w_fc, w_proj, base)


def split_rows(core, value, own, away):
    count, rows = own.shape[0], own.shape[2]
    value = value.astype(BF16)
    half = count * rows
    first = value[:half].reshape(count, 1, rows, -1)
    second = value[half:].reshape(count, 1, rows, -1)

    @pl.when(core == 0)
    def _():
        own[...] = first
        away[...] = second

    @pl.when(core == 1)
    def _():
        own[...] = second
        away[...] = first


def weight_kernel(ids, left, right, own, away):
    split_rows(ids[1], dot(left[...], right[...], 0, 0), own, away)


def weight_pair_kernel(ids, left, right, attn, resid, own, away):
    units = right.shape[1]
    total = dot(attn[0], resid[0], 1, 0)
    for seq in range(1, attn.shape[0]):
        total = total + dot(attn[seq], resid[seq], 1, 0)
    split_rows(ids[1], dot(left[...], right[...], 0, 0), own.at[..., pl.ds(0, units)], away.at[..., pl.ds(0, units)])
    split_rows(ids[1], total, own.at[..., pl.ds(units, total.shape[1])], away.at[..., pl.ds(units, total.shape[1])])


def weight_call(kernel, counts, rows, columns, in_specs, flops, name):
    dp_count, head_count = counts
    spec = pl.BlockSpec((head_count, 1, rows, columns), lambda d, ids: (0, d, 0, 0))
    shape = jax.ShapeDtypeStruct((head_count, dp_count, rows, columns), BF16)
    return pl.pallas_call(
        kernel,
        out_shape=(shape, shape),
        grid_spec=pltpu.PrefetchScalarGridSpec(
            num_scalar_prefetch=1, grid=(dp_count,), in_specs=in_specs, out_specs=(spec, spec)
        ),
        compiler_params=pltpu.CompilerParams(vmem_limit_bytes=VMEM_LIMIT),
        cost_estimate=pl.CostEstimate(
            flops=flops, bytes_accessed=4 * head_count * dp_count * rows * columns, transcendentals=0
        ),
        name=name,
    )


def weight_terms(ids, left, right, counts, rows):
    tokens, columns = right.shape
    span = 2 * counts[1] * rows
    return weight_call(
        weight_kernel,
        counts,
        rows,
        columns,
        [
            pl.BlockSpec((tokens, span), lambda d, ids: (0, d)),
            pl.BlockSpec((tokens, columns), lambda d, ids: (0, 0)),
        ],
        2 * tokens * columns * left.shape[1],
        "weight_terms",
    )(ids, left, right)


def weight_pair_terms(ids, left, right, attn, resid, counts, rows):
    tokens, units = right.shape
    seqs, _, features, seq_tokens = attn.shape
    width = resid.shape[2]
    span = 2 * counts[1] * rows
    return weight_call(
        weight_pair_kernel,
        counts,
        rows,
        units + width,
        [
            pl.BlockSpec((tokens, span), lambda d, ids: (0, d)),
            pl.BlockSpec((tokens, units), lambda d, ids: (0, 0)),
            pl.BlockSpec((seqs, None, features, seq_tokens), lambda d, ids: (0, d ^ ids[2], 0, 0)),
            pl.BlockSpec(resid.shape, lambda d, ids: (0, 0, 0)),
        ],
        2 * tokens * (units + width) * left.shape[1],
        "weight_pair_terms",
    )(ids, left, right, attn, resid)


def to_attention(slots, head):
    count, features, width = slots.shape
    if count == SLOTS:
        return head.reshape(1), slots
    order = jnp.arange(count) ^ head
    natural = slots[order].reshape(count, features, 2, width // 2)
    tokens = natural.transpose(1, 2, 0, 3).reshape(features, 2, SLOTS, -1)
    return jnp.zeros((1,), jnp.int32), tokens.transpose(2, 0, 1, 3).reshape(SLOTS, features, -1)


def from_attention(tokens, head, count):
    if count == SLOTS:
        return tokens
    features = tokens.shape[1]
    natural = tokens.reshape(SLOTS, features, 2, -1).transpose(1, 2, 0, 3)
    natural = natural.reshape(features, 2, count, -1).transpose(2, 0, 1, 3)
    return natural.reshape(count, features, -1)[jnp.arange(count) ^ head]


def on_device(
    stream_in,
    ln1_gain,
    ln1_bias,
    w_qkv,
    b_qv,
    w_out,
    b_out,
    ln2_gain,
    ln2_bias,
    w_fc,
    b_fc,
    w_proj,
    b_proj,
    cotangent,
):
    seq_dev, tok_rows, width = stream_in.shape
    rows = seq_dev * tok_rows
    dp_count, head_count = lax.axis_size("dp"), lax.axis_size("head")
    devices = dp_count * 2 * head_count
    grid = (dp_count, 2, head_count)
    dp, core, head = lax.axis_index("dp"), lax.axis_index("blk"), lax.axis_index("head")
    ids = jnp.stack([dp, core, head]).astype(jnp.int32)
    group = width // head_count
    heads = group // HD
    own_rows = w_qkv.shape[0]
    hidden_width = w_fc.shape[1]

    sizes = [own_rows] * 8 + [b_fc.shape[0]]
    small = jnp.concatenate(
        [ln1_gain, ln1_bias, b_qv[0], b_qv[1], b_out, ln2_gain, ln2_bias, b_proj, b_fc]
    ).astype(F32)
    small = gather_small(small, ids)
    edges = [sum(sizes[:i]) for i in range(len(sizes) + 1)]
    full = [small[:, edges[i] : edges[i + 1]].reshape(-1) for i in range(len(sizes))]
    gain_one, bias_one, bias_q, bias_v, bias_out, gain_two, bias_two, bias_proj, bias_fc = full

    square = head_count == 4
    stream_rows = stream_in.reshape(rows, width)
    normed_one, inv_one = normalize(stream_rows)
    act_one = (normed_one * gain_one + bias_one).astype(BF16).reshape(seq_dev, tok_rows, width)

    columns = w_qkv.reshape(own_rows, 3, head_count, group)
    parts = [
        pick(columns, head ^ slot, 2).reshape(own_rows, 3 * group) for slot in range(head_count)
    ]
    parts = [parts[0]] + [to_xor(parts[slot], slot) for slot in range(1, head_count)]
    one_z = gather_dp(jnp.concatenate([w_fc, w_out], axis=1))
    two_z = gather_dp(w_proj)

    own_half = by_half(core, pick(act_one, core), to_other_core(pick(act_one, 1 - core)))
    own_half = own_half.reshape(2 * tok_rows, width)
    own_half, shard = together(own_half, jnp.concatenate(parts, axis=1))
    group_z = gather_z(shard)
    group_z = jnp.stack([pick(group_z, (dp + dp_count - k) % dp_count) for k in range(dp_count)])
    wide = 3 * group
    (group_w,) = place(
        [group_z[:, :, slot * wide : (slot + 1) * wide] for slot in range(head_count)],
        (wide,),
        ids,
    )
    acts = plane_far(own_half, plane_near(own_half), 0) if square else gather_plane(own_half)
    *acts, one_z = together(*acts, one_z)
    one_near = plane_near(one_z) if square else gather_plane(one_z)
    qkv_bias = jnp.concatenate(
        [
            pick(bias_q.reshape(head_count, group), head),
            jnp.zeros((group,), F32),
            pick(bias_v.reshape(head_count, group), head),
        ]
    )[:, None]
    qkv_slots = jnp.stack([(dot(group_w, act, 0, 1) + qkv_bias).astype(BF16) for act in acts])
    me, qkv = to_attention(qkv_slots, head)
    qkv = qkv.reshape(SLOTS, 3, heads, HD, -1)
    attn, lse = attend(me, qkv)
    attn, two_z, *one_near = together(attn, two_z, *one_near)
    attn_slots = from_attention(attn.reshape(SLOTS, group, -1), head, head_count)
    attn_all = [attn_slots[0]] + [to_xor(attn_slots[j], j) for j in range(1, head_count)]
    one_pieces = plane_far(one_z, one_near, 2) if square else one_near
    attn_all = jnp.stack(attn_all)
    first, second = attn_all[:, :, :tok_rows], attn_all[:, :, tok_rows:]
    keep = jnp.where(core == 0, first, second)
    away = jnp.where(core == 0, second, first)
    attn_cols = by_half(core, keep, to_other_core(away))

    attn_cols, two_z, *one_pieces = together(attn_cols, two_z, *one_pieces)
    two_near = plane_near(two_z) if square else gather_plane(two_z)
    full_wfc, full_wout = place(one_pieces, (hidden_width, width), ids)
    slot_wout = full_wout.reshape(head_count, group, width)
    slot_wout = jnp.stack([pick(slot_wout, head ^ slot) for slot in range(head_count)])

    resid = (
        stream_rows
        + jnp.einsum("sjdt,jde->ste", attn_cols, slot_wout, preferred_element_type=F32).reshape(
            rows, width
        )
        + bias_out
    )
    normed_two, inv_two = normalize(resid)
    ctx = (normed_two * gain_two + bias_two).astype(BF16)
    ctx, *two_near = together(ctx, *two_near)
    two_pieces = plane_far(two_z, two_near, 1) if square else two_near
    hidden, slope = feed(ctx, full_wfc, bias_fc)
    hidden, *two_pieces = together(hidden, *two_pieces)
    cot_rows = cotangent.reshape(rows, width)
    cot_low = cot_rows.astype(BF16)
    grad_b_proj = jnp.sum(cot_rows, axis=0)
    chips = (dp_count, head_count)
    aligned = group == 2 * head_count * own_rows and (head_count * own_rows) % 128 == 0
    if aligned:
        two_own, two_away = weight_terms(ids, hidden, cot_low, chips, w_proj.shape[0])
    else:
        two_own, two_away = split_terms(
            dot(hidden, cot_low, 0, 0).astype(BF16).reshape(grid + (-1, width)), core
        )
    two_terms = chip_terms(two_own, two_away)
    (full_wproj,) = place(two_pieces, (width,), ids)
    two_terms, cot_low = together(two_terms, cot_low)
    two_plane = scatter_plane(two_terms)
    pre_low, grad_b_fc, grad_ctx, stream_out = feed_back(
        cot_low, hidden, slope, full_wfc, full_wproj, resid + bias_proj
    )
    grad_b_fc = grad_b_fc.reshape(-1)
    grad_ln2_gain = jnp.sum(grad_ctx * normed_two, axis=0)
    grad_ln2_bias = jnp.sum(grad_ctx, axis=0)
    grad_resid = cot_rows + norm_back(grad_ctx * gain_two, normed_two, inv_two)
    grad_b_out = jnp.sum(grad_resid, axis=0)
    resid_low = grad_resid.astype(BF16)
    resid_three = resid_low.reshape(seq_dev, tok_rows, width)
    grad_attn_cols = jnp.einsum(
        "ste,jde->sjdt", resid_three, slot_wout, preferred_element_type=F32
    ).astype(BF16)
    kept = pick(grad_attn_cols, core)
    arrived = to_other_core(pick(grad_attn_cols, 1 - core))
    grad_half = jnp.where(
        core == 0,
        jnp.concatenate([kept, arrived], axis=2),
        jnp.concatenate([arrived, kept], axis=2),
    )
    grad_half, two_plane = together(grad_half, two_plane)
    shard_wproj = scatter_dp(two_plane)
    grad_slots = [grad_half[0]] + [to_xor(grad_half[j], j) for j in range(1, head_count)]

    if aligned:
        one_own, one_away = weight_pair_terms(
            ids, ctx, pre_low, attn_cols, resid_three, chips, own_rows
        )
    else:
        grad_w_fc = dot(ctx, pre_low, 0, 0).astype(BF16)
        grad_w_out = jnp.einsum(
            "sjdt,ste->jde", attn_cols, resid_three, preferred_element_type=F32
        ).astype(BF16)
        grad_w_out = jnp.stack([pick(grad_w_out, head ^ slot) for slot in range(head_count)])
        one_own, one_away = split_terms(
            jnp.concatenate(
                [
                    grad_w_fc.reshape(grid + (-1, hidden_width)),
                    grad_w_out.reshape(grid + (-1, width)),
                ],
                axis=4,
            ),
            core,
        )
    one_terms = chip_terms(one_own, one_away)
    *grad_slots, one_terms = together(*grad_slots, one_terms)
    one_plane = scatter_plane(one_terms)

    _, grad_attn = to_attention(jnp.stack(grad_slots), head)
    grad_attn = grad_attn.reshape(SLOTS, heads, HD, -1)
    grad_qkv = attend_back(me, qkv, attn, grad_attn, lse)
    grad_qkv, shard_wproj = together(grad_qkv, shard_wproj)
    grad_qkv = from_attention(grad_qkv.reshape(SLOTS, 3 * group, -1), head, head_count)

    act_parts = [dot(grad_qkv[slot], group_w, 0, 1) for slot in range(head_count)]
    act_parts = [act_parts[0]] + [part.astype(BF16) for part in act_parts[1:]]
    act_terms = [to_xor(act_parts[j], j) for j in range(1, head_count)]
    grad_group_w = dot(acts[0], grad_qkv[0], 0, 1)
    for slot in range(1, head_count):
        grad_group_w = grad_group_w + dot(acts[slot], grad_qkv[slot], 0, 1)
    token_sums = jnp.sum(grad_qkv.astype(F32), axis=(0, 2)).reshape(3, group)
    grad_bias = jnp.zeros((3, head_count, group), F32)
    grad_bias = lax.dynamic_update_index_in_dim(grad_bias, token_sums, head, 1).reshape(3, width)

    wide_w = group_w.astype(F32)
    act_sum = jnp.sum(wide_w * token_sums.reshape(1, -1), axis=1)
    act_product = jnp.sum(wide_w * grad_group_w, axis=1)
    vectors = [
        act_product,
        act_sum,
        grad_bias[0],
        grad_bias[2],
        grad_b_out,
        grad_ln2_gain,
        grad_ln2_bias,
        grad_b_proj,
        grad_b_fc,
    ]
    packed = jnp.concatenate([v.reshape(devices, -1) for v in vectors], axis=1)
    mine = scatter_small(packed.reshape(grid + (-1,)), core, head, dp)
    grad_group_w = grad_group_w.astype(BF16).reshape(grid + (own_rows, 3 * group))
    half_w = pick(grad_group_w, core, 1).astype(F32) + core_terms(grad_group_w, core).astype(F32)
    shard_w = scatter_z(half_w, dp)
    *near_terms, shard_w, one_plane = together(*act_terms[:2], shard_w, one_plane)
    act_terms = near_terms + act_terms[2:]
    mine, shard_one, *act_terms = together(mine, scatter_dp(one_plane), *act_terms)
    sums = plane_total(act_parts[0], act_terms).reshape(2, tok_rows, width)
    grad_act = by_half(
        core, pick(sums, core), to_other_core(pick(sums, 1 - core))
    ).reshape(rows, width)

    pieces = jnp.stack(
        [pick(shard_w, head)]
        + [to_xor(pick(shard_w, head ^ slot), slot) for slot in range(1, head_count)]
    )
    ordered = [pick(pieces, head ^ slot) for slot in range(head_count)]
    shard_wqkv = jnp.concatenate(
        [piece[:, c * group : (c + 1) * group] for c in range(3) for piece in ordered], axis=1
    )

    shard_wfc, shard_wout = shard_one[:, :hidden_width], shard_one[:, hidden_width:]
    grad_rows_in = grad_resid + norm_back(grad_act * gain_one, normed_one, inv_one)

    cut = [mine[edges[i] : edges[i + 1]] for i in range(len(sizes))]
    return (
        stream_out.reshape(seq_dev, tok_rows, width),
        grad_rows_in.reshape(seq_dev, tok_rows, width),
        (cut[0] - ln1_bias.astype(F32) * cut[1]) / ln1_gain.astype(F32),
        cut[1],
        shard_wqkv,
        jnp.stack([cut[2], cut[3]]),
        shard_wout.reshape(-1, width),
        cut[4],
        cut[5],
        cut[6],
        shard_wfc.reshape(-1, hidden_width),
        cut[8],
        shard_wproj.reshape(-1, width),
        cut[7],
    )


def solution(mesh):
    every = ("dp", "blk", "head")
    tokens = P("dp", ("blk", "head"), None)
    vector, matrix = P(every), P(every, None)
    in_specs = (
        tokens,
        vector,
        vector,
        matrix,
        P(None, every),
        matrix,
        vector,
        vector,
        vector,
        matrix,
        vector,
        matrix,
        vector,
        tokens,
    )
    out_specs = (
        tokens,
        tokens,
        vector,
        vector,
        matrix,
        P(None, every),
        matrix,
        vector,
        vector,
        vector,
        matrix,
        vector,
        matrix,
        vector,
    )
    return jax.shard_map(
        on_device, mesh=mesh, in_specs=in_specs, out_specs=out_specs, check_vma=False
    )
```

```python
import functools
import math

import jax
import jax.numpy as jnp
from jax import lax
from jax.experimental import pallas as pl
from jax.experimental.pallas import tpu as pltpu
from jax.sharding import PartitionSpec as P

HD = 64
EPSILON = 1e-05
GELU_COEF = 0.044715
ROOT_TWO_PI = math.sqrt(2.0 / math.pi)
SCALE = 1.0 / math.sqrt(HD)
LOG2E = math.log2(math.e)
F32 = jnp.float32
BF16 = jnp.bfloat16
VMEM_LIMIT = 48 * 1024 * 1024


def normalize(stream):
    centred = stream - jnp.mean(stream, axis=-1, keepdims=True)
    inv_std = lax.rsqrt(jnp.mean(centred * centred, axis=-1, keepdims=True) + EPSILON)
    return (centred * inv_std, inv_std)


def norm_back(grad_normed, normed, inv_std):
    return inv_std * (
        grad_normed
        - jnp.mean(grad_normed, axis=-1, keepdims=True)
        - normed * jnp.mean(grad_normed * normed, axis=-1, keepdims=True)
    )


def gelu_pair(pre_act):
    square = pre_act * pre_act
    upper = 0.5 + 0.5 * jnp.tanh(pre_act * (ROOT_TWO_PI + (ROOT_TWO_PI * GELU_COEF) * square))
    bend = 2.0 * ROOT_TWO_PI + (6.0 * ROOT_TWO_PI * GELU_COEF) * square
    return (pre_act * upper, upper + upper * (pre_act * (1.0 - upper)) * bend)


def dot(left, right, left_dim, right_dim):
    return lax.dot_general(
        left, right, (((left_dim,), (right_dim,)), ((), ())), preferred_element_type=F32
    )


def to_xor(value, step):
    count = lax.axis_size("head")
    return lax.ppermute(value, "head", [(i, i ^ step) for i in range(count)])


def to_shift(value, step):
    count = lax.axis_size("dp")
    return lax.ppermute(value, "dp", [(i, (i + step) % count) for i in range(count)])


def to_other_core(value):
    return lax.ppermute(value, "blk", [(0, 1), (1, 0)])


def pick(stacked, index, axis=0):
    return lax.dynamic_index_in_dim(stacked, index, axis, keepdims=False)


def by_half(core, own, other):
    return jnp.where(core == 0, jnp.stack([own, other]), jnp.stack([other, own]))


def place_kernel(widths, ids, *refs):
    count = (len(refs) - 1 - len(widths)) // 2
    pieces, outs, sem = refs[: 2 * count], refs[2 * count : -1], refs[-1]
    core, head = ids[1], ids[2]
    copies = []
    for which in range(2):
        for slot in range(count):
            start = 0
            for out, columns in zip(outs, widths):
                copies.append(
                    pltpu.make_async_copy(
                        pieces[which * count + slot].at[:, :, pl.ds(start, columns)],
                        out.at[:, core ^ which, head ^ slot],
                        sem.at[len(copies)],
                    )
                )
                start += columns
    for copy in copies:
        copy.start()
    for copy in copies:
        copy.wait()


def place(mine, widths, ids):
    dp_count, rows, _ = mine[0].shape
    pieces = list(mine) + [to_other_core(piece) for piece in mine]
    shapes = [(dp_count, 2, len(mine), rows, columns) for columns in widths]
    outs = pl.pallas_call(
        functools.partial(place_kernel, widths),
        out_shape=[jax.ShapeDtypeStruct(shape, BF16) for shape in shapes],
        grid_spec=pltpu.PrefetchScalarGridSpec(
            num_scalar_prefetch=1,
            grid=(1,),
            in_specs=[pl.BlockSpec(memory_space=pl.ANY)] * len(pieces),
            out_specs=[
                pl.BlockSpec(
                    shape, lambda i, ids: (0, 0, 0, 0, 0), pipeline_mode=pl.Buffered(1)
                )
                for shape in shapes
            ],
            scratch_shapes=[pltpu.SemaphoreType.DMA((len(pieces) * len(widths),))],
        ),
        compiler_params=pltpu.CompilerParams(vmem_limit_bytes=VMEM_LIMIT),
        name="place",
    )(ids, *pieces)
    return [out.reshape(-1, columns) for out, columns in zip(outs, widths)]


def gather_dp(shard):
    full = lax.all_gather(shard, "dp", axis=0, tiled=True)
    return full.reshape((-1,) + shard.shape)


def split_terms(grad, core):
    return (
        pick(grad, core, 1).transpose(1, 0, 2, 3),
        pick(grad, 1 - core, 1).transpose(1, 0, 2, 3),
    )


def chip_terms(own, away):
    total = (own.astype(F32) + to_other_core(away).astype(F32)).astype(BF16)
    return total.reshape(-1, total.shape[-1])


def scatter_plane(terms):
    return lax.psum_scatter(terms, "head", scatter_dimension=0, tiled=True)


def scatter_dp(terms):
    return lax.psum_scatter(terms, "dp", scatter_dimension=0, tiled=True)


def gather_z(shard):
    return jnp.stack([shard] + [to_shift(shard, k) for k in range(1, lax.axis_size("dp"))])


def gather_plane(own):
    return [own] + [to_xor(own, j) for j in range(1, lax.axis_size("head"))]


def plane_near(own):
    return to_xor(own, 1), to_xor(own, 2)


def plane_far(own, near, axis):
    half = own.shape[axis] // 2
    lower = to_xor(lax.slice_in_dim(near[0], 0, half, axis=axis), 2)
    upper = to_xor(lax.slice_in_dim(near[1], half, 2 * half, axis=axis), 1)
    return [own, near[0], near[1], jnp.concatenate([lower, upper], axis=axis)]


def core_terms(grad, core):
    return to_other_core(pick(grad, 1 - core, 1))


def plane_total(own, terms):
    total = own
    for piece in terms:
        total = total + piece.astype(F32)
    return total


def scatter_z(total, dp):
    dp_count = total.shape[0]
    low = total.astype(BF16)
    result = pick(total, dp)
    for step in range(1, dp_count):
        result = result + to_shift(pick(low, lax.rem(dp + step, dp_count)), step).astype(F32)
    return result


def together(*values):
    return lax.optimization_barrier(values)


def gather_small(vector, ids):
    dp_count, head_count = lax.axis_size("dp"), lax.axis_size("head")
    rows = gather_z(vector[None])
    rows = jnp.stack(gather_plane(rows))
    rows = jnp.stack([rows, to_other_core(rows)])
    total = 2 * head_count * dp_count
    slot = jnp.arange(total)
    which, plane, step = slot // (head_count * dp_count), (slot // dp_count) % head_count, slot % dp_count
    source = ((ids[0] - step) % dp_count) * 2 * head_count + (ids[1] ^ which) * head_count + (ids[2] ^ plane)
    chosen = (source[None, :] == jnp.arange(total)[:, None]).astype(F32)
    return jnp.dot(chosen, rows.reshape(total, -1), precision=lax.Precision.HIGHEST)


def scatter_small(rows, core, head, dp):
    dp_count, _, head_count = rows.shape[:3]
    half = pick(rows, core, 1) + to_other_core(pick(rows, 1 - core, 1))
    total = pick(half, head, 1)
    for slot in range(1, head_count):
        total = total + to_xor(pick(half, head ^ slot, 1), slot)
    result = pick(total, dp)
    for step in range(1, dp_count):
        result = result + to_shift(pick(total, lax.rem(dp + step, dp_count)), step)
    return result


SLOTS = 4


def causal(block):
    key = lax.broadcasted_iota(jnp.int32, (block, block), 0)
    query = lax.broadcasted_iota(jnp.int32, (block, block), 1)
    return key <= query


def forward_kernel(block, me_ref, qkv, out, lse, scores_a, scores_b):
    me = me_ref[0]
    factor = SCALE * LOG2E
    mask = causal(block)

    def part(which, pos):
        return qkv[(pos % SLOTS) ^ me, which, :, pl.ds((pos // SLOTS) * block, block)]

    for row in range(2 * SLOTS):
        scores = scores_a if row % 2 == 0 else scores_b
        query = part(0, row)
        top = None
        for col in range(row + 1):
            tile = dot(part(1, col), query, 0, 0)
            if col == row:
                tile = jnp.where(mask, tile, -jnp.inf)
            scores[pl.ds(col * block, block), :] = tile
            high = jnp.max(tile, axis=0, keepdims=True)
            top = high if top is None else jnp.maximum(top, high)
        shift = top * factor
        total = jnp.zeros_like(top)
        result = jnp.zeros((HD, block), F32)
        for col in range(row + 1):
            probs = jnp.exp2(scores[pl.ds(col * block, block), :] * factor - shift)
            total = total + jnp.sum(probs, axis=0, keepdims=True)
            result = result + dot(part(2, col), probs.astype(BF16), 1, 0)
        out[(row % SLOTS) ^ me, :, pl.ds((row // SLOTS) * block, block)] = (result / total).astype(BF16)
        lse[pl.ds(row, 1), :] = shift + jnp.log2(total)


def backward_kernel(block, me_ref, qkv, attn, grad_attn, lse, out, grad_q, delta):
    me = me_ref[0]
    factor = SCALE * LOG2E
    mask = causal(block)

    def part(which, pos):
        return qkv[(pos % SLOTS) ^ me, which, :, pl.ds((pos // SLOTS) * block, block)]

    def tokens(ref, pos):
        return ref[(pos % SLOTS) ^ me, :, pl.ds((pos // SLOTS) * block, block)]

    for row in range(2 * SLOTS):
        product = tokens(grad_attn, row).astype(F32) * tokens(attn, row).astype(F32)
        delta[pl.ds(row, 1), :] = jnp.sum(product, axis=0, keepdims=True)
    for col in range(2 * SLOTS):
        key, value = part(1, col), part(2, col)
        grad_key = jnp.zeros((HD, block), F32)
        grad_value = jnp.zeros((HD, block), F32)
        for row in range(col, 2 * SLOTS):
            query, grad_row = part(0, row), tokens(grad_attn, row)
            probs = jnp.exp2(dot(key, query, 0, 0) * factor - lse[pl.ds(row, 1), :])
            if row == col:
                probs = jnp.where(mask, probs, 0.0)
            grad_probs = dot(value, grad_row, 0, 0)
            grad_scores = (probs * (grad_probs - delta[pl.ds(row, 1), :])).astype(BF16)
            grad_value = grad_value + dot(grad_row, probs.astype(BF16), 1, 1)
            grad_key = grad_key + dot(query, grad_scores, 1, 1)
            term = dot(key, grad_scores, 1, 0)
            if col == 0:
                grad_q[row] = term
            else:
                grad_q[row] += term
        where = ((col % SLOTS) ^ me, pl.ds((col // SLOTS) * block, block))
        out[where[0], 1, :, where[1]] = (grad_key * SCALE).astype(BF16)
        out[where[0], 2, :, where[1]] = grad_value.astype(BF16)
    for row in range(2 * SLOTS):
        where = ((row % SLOTS) ^ me, pl.ds((row // SLOTS) * block, block))
        out[where[0], 0, :, where[1]] = (grad_q[row] * SCALE).astype(BF16)


def head_spec(width):
    return pl.BlockSpec((SLOTS, None, HD, width), lambda h, me: (0, h, 0, 0))


def triple_spec(width):
    return pl.BlockSpec((SLOTS, 3, None, HD, width), lambda h, me: (0, 0, h, 0, 0))


def attend(me, qkv):
    heads, width = qkv.shape[2], qkv.shape[4]
    block = width // 2
    length = SLOTS * width
    return pl.pallas_call(
        functools.partial(forward_kernel, block),
        out_shape=(
            jax.ShapeDtypeStruct((SLOTS, heads, HD, width), BF16),
            jax.ShapeDtypeStruct((heads, 2 * SLOTS, block), F32),
        ),
        grid_spec=pltpu.PrefetchScalarGridSpec(
            num_scalar_prefetch=1,
            grid=(heads,),
            in_specs=[triple_spec(width)],
            out_specs=(
                head_spec(width),
                pl.BlockSpec((None, 2 * SLOTS, block), lambda h, me: (h, 0, 0)),
            ),
            scratch_shapes=[pltpu.VMEM((length, block), F32)] * 2,
        ),
        compiler_params=pltpu.CompilerParams(vmem_limit_bytes=VMEM_LIMIT),
        cost_estimate=pl.CostEstimate(
            flops=2 * heads * length * length * HD,
            bytes_accessed=8 * heads * HD * length,
            transcendentals=heads * length * length // 2,
        ),
        name="attend",
    )(me, qkv)


def attend_back(me, qkv, attn, grad_attn, lse):
    heads, width = qkv.shape[2], qkv.shape[4]
    block = width // 2
    length = SLOTS * width
    return pl.pallas_call(
        functools.partial(backward_kernel, block),
        out_shape=jax.ShapeDtypeStruct(qkv.shape, BF16),
        grid_spec=pltpu.PrefetchScalarGridSpec(
            num_scalar_prefetch=1,
            grid=(heads,),
            in_specs=[
                triple_spec(width),
                head_spec(width),
                head_spec(width),
                pl.BlockSpec((None, 2 * SLOTS, block), lambda h, me: (h, 0, 0)),
            ],
            out_specs=triple_spec(width),
            scratch_shapes=[
                pltpu.VMEM((2 * SLOTS, HD, block), F32),
                pltpu.VMEM((2 * SLOTS, block), F32),
            ],
        ),
        compiler_params=pltpu.CompilerParams(vmem_limit_bytes=VMEM_LIMIT),
        cost_estimate=pl.CostEstimate(
            flops=5 * heads * length * length * HD,
            bytes_accessed=16 * heads * HD * length,
            transcendentals=heads * length * length // 2,
        ),
        name="attend_back",
    )(me, qkv, attn, grad_attn, lse)


def feed_kernel(ctx, weight, bias, hidden, slope):
    pre = dot(ctx[...], weight[...], 1, 0) + bias[...]
    value, steep = gelu_pair(pre)
    hidden[...] = value.astype(BF16)
    slope[...] = steep


def feed(ctx, weight, bias):
    rows, width = ctx.shape
    units = weight.shape[1]
    block = min(512, units)
    return pl.pallas_call(
        feed_kernel,
        out_shape=(
            jax.ShapeDtypeStruct((rows, units), BF16),
            jax.ShapeDtypeStruct((rows, units), F32),
        ),
        grid=(units // block,),
        in_specs=[
            pl.BlockSpec((rows, width), lambda i: (0, 0)),
            pl.BlockSpec((width, block), lambda i: (0, i)),
            pl.BlockSpec((1, block), lambda i: (0, i)),
        ],
        out_specs=(
            pl.BlockSpec((rows, block), lambda i: (0, i)),
            pl.BlockSpec((rows, block), lambda i: (0, i)),
        ),
        compiler_params=pltpu.CompilerParams(vmem_limit_bytes=VMEM_LIMIT),
        cost_estimate=pl.CostEstimate(
            flops=2 * rows * width * units,
            bytes_accessed=2 * width * units + 6 * rows * units,
            transcendentals=rows * units,
        ),
        name="feed",
    )(ctx, weight, bias.reshape(1, -1))


def feed_back_kernel(
    cot, hidden, slope, w_fc, w_proj, base, pre_low, grad_bias, grad_ctx, stream, sum_ctx, sum_out
):
    step = pl.program_id(0)
    grad_pre = dot(cot[...], w_proj[...], 1, 1) * slope[...]
    grad_bias[...] = jnp.sum(grad_pre, axis=0, keepdims=True)
    low = grad_pre.astype(BF16)
    pre_low[...] = low
    back = dot(low, w_fc[...], 1, 1)
    ahead = dot(hidden[...], w_proj[...], 1, 0)

    @pl.when(step == 0)
    def _():
        sum_ctx[...] = back
        sum_out[...] = base[...] + ahead

    @pl.when(step > 0)
    def _():
        sum_ctx[...] += back
        sum_out[...] += ahead

    @pl.when(step == pl.num_programs(0) - 1)
    def _():
        grad_ctx[...] = sum_ctx[...]
        stream[...] = sum_out[...]


def feed_back(cot, hidden, slope, w_fc, w_proj, base):
    rows, width = cot.shape
    units = hidden.shape[1]
    block = min(1024, units)
    whole = pl.BlockSpec((rows, width), lambda i: (0, 0))
    columns = pl.BlockSpec((rows, block), lambda i: (0, i))
    return pl.pallas_call(
        feed_back_kernel,
        out_shape=(
            jax.ShapeDtypeStruct((rows, units), BF16),
            jax.ShapeDtypeStruct((1, units), F32),
            jax.ShapeDtypeStruct((rows, width), F32),
            jax.ShapeDtypeStruct((rows, width), F32),
        ),
        grid=(units // block,),
        in_specs=[
            whole,
            columns,
            columns,
            pl.BlockSpec((width, block), lambda i: (0, i)),
            pl.BlockSpec((block, width), lambda i: (i, 0)),
            whole,
        ],
        out_specs=(columns, pl.BlockSpec((1, block), lambda i: (0, i)), whole, whole),
        scratch_shapes=[pltpu.VMEM((rows, width), F32)] * 2,
        compiler_params=pltpu.CompilerParams(vmem_limit_bytes=VMEM_LIMIT),
        cost_estimate=pl.CostEstimate(
            flops=6 * rows * width * units,
            bytes_accessed=4 * width * units + 8 * rows * units,
            transcendentals=0,
        ),
        name="feed_back",
    )(cot, hidden, slope, w_fc, w_proj, base)


def split_rows(core, value, own, away):
    count, rows = own.shape[0], own.shape[2]
    value = value.astype(BF16)
    half = count * rows
    first = value[:half].reshape(count, 1, rows, -1)
    second = value[half:].reshape(count, 1, rows, -1)

    @pl.when(core == 0)
    def _():
        own[...] = first
        away[...] = second

    @pl.when(core == 1)
    def _():
        own[...] = second
        away[...] = first


def weight_kernel(ids, left, right, own, away):
    split_rows(ids[1], dot(left[...], right[...], 0, 0), own, away)


def weight_pair_kernel(ids, left, right, attn, resid, own, away):
    units = right.shape[1]
    total = dot(attn[0], resid[0], 1, 0)
    for seq in range(1, attn.shape[0]):
        total = total + dot(attn[seq], resid[seq], 1, 0)
    split_rows(ids[1], dot(left[...], right[...], 0, 0), own.at[..., pl.ds(0, units)], away.at[..., pl.ds(0, units)])
    split_rows(ids[1], total, own.at[..., pl.ds(units, total.shape[1])], away.at[..., pl.ds(units, total.shape[1])])


def weight_call(kernel, counts, rows, columns, in_specs, flops, name):
    dp_count, head_count = counts
    spec = pl.BlockSpec((head_count, 1, rows, columns), lambda d, ids: (0, d, 0, 0))
    shape = jax.ShapeDtypeStruct((head_count, dp_count, rows, columns), BF16)
    return pl.pallas_call(
        kernel,
        out_shape=(shape, shape),
        grid_spec=pltpu.PrefetchScalarGridSpec(
            num_scalar_prefetch=1, grid=(dp_count,), in_specs=in_specs, out_specs=(spec, spec)
        ),
        compiler_params=pltpu.CompilerParams(vmem_limit_bytes=VMEM_LIMIT),
        cost_estimate=pl.CostEstimate(
            flops=flops, bytes_accessed=4 * head_count * dp_count * rows * columns, transcendentals=0
        ),
        name=name,
    )


def weight_terms(ids, left, right, counts, rows):
    tokens, columns = right.shape
    span = 2 * counts[1] * rows
    return weight_call(
        weight_kernel,
        counts,
        rows,
        columns,
        [
            pl.BlockSpec((tokens, span), lambda d, ids: (0, d)),
            pl.BlockSpec((tokens, columns), lambda d, ids: (0, 0)),
        ],
        2 * tokens * columns * left.shape[1],
        "weight_terms",
    )(ids, left, right)


def weight_pair_terms(ids, left, right, attn, resid, counts, rows):
    tokens, units = right.shape
    seqs, _, features, seq_tokens = attn.shape
    width = resid.shape[2]
    span = 2 * counts[1] * rows
    return weight_call(
        weight_pair_kernel,
        counts,
        rows,
        units + width,
        [
            pl.BlockSpec((tokens, span), lambda d, ids: (0, d)),
            pl.BlockSpec((tokens, units), lambda d, ids: (0, 0)),
            pl.BlockSpec((seqs, None, features, seq_tokens), lambda d, ids: (0, d ^ ids[2], 0, 0)),
            pl.BlockSpec(resid.shape, lambda d, ids: (0, 0, 0)),
        ],
        2 * tokens * (units + width) * left.shape[1],
        "weight_pair_terms",
    )(ids, left, right, attn, resid)


def to_attention(slots, head):
    count, features, width = slots.shape
    if count == SLOTS:
        return head.reshape(1), slots
    order = jnp.arange(count) ^ head
    natural = slots[order].reshape(count, features, 2, width // 2)
    tokens = natural.transpose(1, 2, 0, 3).reshape(features, 2, SLOTS, -1)
    return jnp.zeros((1,), jnp.int32), tokens.transpose(2, 0, 1, 3).reshape(SLOTS, features, -1)


def from_attention(tokens, head, count):
    if count == SLOTS:
        return tokens
    features = tokens.shape[1]
    natural = tokens.reshape(SLOTS, features, 2, -1).transpose(1, 2, 0, 3)
    natural = natural.reshape(features, 2, count, -1).transpose(2, 0, 1, 3)
    return natural.reshape(count, features, -1)[jnp.arange(count) ^ head]


def on_device(
    stream_in,
    ln1_gain,
    ln1_bias,
    w_qkv,
    b_qv,
    w_out,
    b_out,
    ln2_gain,
    ln2_bias,
    w_fc,
    b_fc,
    w_proj,
    b_proj,
    cotangent,
):
    seq_dev, tok_rows, width = stream_in.shape
    rows = seq_dev * tok_rows
    dp_count, head_count = lax.axis_size("dp"), lax.axis_size("head")
    devices = dp_count * 2 * head_count
    grid = (dp_count, 2, head_count)
    dp, core, head = lax.axis_index("dp"), lax.axis_index("blk"), lax.axis_index("head")
    ids = jnp.stack([dp, core, head]).astype(jnp.int32)
    group = width // head_count
    heads = group // HD
    own_rows = w_qkv.shape[0]
    hidden_width = w_fc.shape[1]

    sizes = [own_rows] * 8 + [b_fc.shape[0]]
    small = jnp.concatenate(
        [ln1_gain, ln1_bias, b_qv[0], b_qv[1], b_out, ln2_gain, ln2_bias, b_proj, b_fc]
    ).astype(F32)
    small = gather_small(small, ids)
    edges = [sum(sizes[:i]) for i in range(len(sizes) + 1)]
    full = [small[:, edges[i] : edges[i + 1]].reshape(-1) for i in range(len(sizes))]
    gain_one, bias_one, bias_q, bias_v, bias_out, gain_two, bias_two, bias_proj, bias_fc = full

    square = head_count == 4
    stream_rows = stream_in.reshape(rows, width)
    normed_one, inv_one = normalize(stream_rows)
    act_one = (normed_one * gain_one + bias_one).astype(BF16).reshape(seq_dev, tok_rows, width)

    columns = w_qkv.reshape(own_rows, 3, head_count, group)
    parts = [
        pick(columns, head ^ slot, 2).reshape(own_rows, 3 * group) for slot in range(head_count)
    ]
    parts = [parts[0]] + [to_xor(parts[slot], slot) for slot in range(1, head_count)]
    one_z = gather_dp(jnp.concatenate([w_fc, w_out], axis=1))
    two_z = gather_dp(w_proj)

    own_half = by_half(core, pick(act_one, core), to_other_core(pick(act_one, 1 - core)))
    own_half = own_half.reshape(2 * tok_rows, width)
    own_half, shard = together(own_half, jnp.concatenate(parts, axis=1))
    group_z = gather_z(shard)
    group_z = jnp.stack([pick(group_z, (dp + dp_count - k) % dp_count) for k in range(dp_count)])
    wide = 3 * group
    (group_w,) = place(
        [group_z[:, :, slot * wide : (slot + 1) * wide] for slot in range(head_count)],
        (wide,),
        ids,
    )
    acts = plane_far(own_half, plane_near(own_half), 0) if square else gather_plane(own_half)
    *acts, one_z = together(*acts, one_z)
    one_near = plane_near(one_z) if square else gather_plane(one_z)
    qkv_bias = jnp.concatenate(
        [
            pick(bias_q.reshape(head_count, group), head),
            jnp.zeros((group,), F32),
            pick(bias_v.reshape(head_count, group), head),
        ]
    )[:, None]
    qkv_slots = jnp.stack([(dot(group_w, act, 0, 1) + qkv_bias).astype(BF16) for act in acts])
    me, qkv = to_attention(qkv_slots, head)
    qkv = qkv.reshape(SLOTS, 3, heads, HD, -1)
    attn, lse = attend(me, qkv)
    attn, two_z, *one_near = together(attn, two_z, *one_near)
    attn_slots = from_attention(attn.reshape(SLOTS, group, -1), head, head_count)
    attn_all = [attn_slots[0]] + [to_xor(attn_slots[j], j) for j in range(1, head_count)]
    one_pieces = plane_far(one_z, one_near, 2) if square else one_near
    attn_all = jnp.stack(attn_all)
    first, second = attn_all[:, :, :tok_rows], attn_all[:, :, tok_rows:]
    keep = jnp.where(core == 0, first, second)
    away = jnp.where(core == 0, second, first)
    attn_cols = by_half(core, keep, to_other_core(away))

    attn_cols, two_z, *one_pieces = together(attn_cols, two_z, *one_pieces)
    two_near = plane_near(two_z) if square else gather_plane(two_z)
    full_wfc, full_wout = place(one_pieces, (hidden_width, width), ids)
    slot_wout = full_wout.reshape(head_count, group, width)
    slot_wout = jnp.stack([pick(slot_wout, head ^ slot) for slot in range(head_count)])

    resid = (
        stream_rows
        + jnp.einsum("sjdt,jde->ste", attn_cols, slot_wout, preferred_element_type=F32).reshape(
            rows, width
        )
        + bias_out
    )
    normed_two, inv_two = normalize(resid)
    ctx = (normed_two * gain_two + bias_two).astype(BF16)
    ctx, *two_near = together(ctx, *two_near)
    two_pieces = plane_far(two_z, two_near, 1) if square else two_near
    hidden, slope = feed(ctx, full_wfc, bias_fc)
    hidden, *two_pieces = together(hidden, *two_pieces)
    cot_rows = cotangent.reshape(rows, width)
    cot_low = cot_rows.astype(BF16)
    grad_b_proj = jnp.sum(cot_rows, axis=0)
    chips = (dp_count, head_count)
    aligned = group == 2 * head_count * own_rows and (head_count * own_rows) % 128 == 0
    if aligned:
        two_own, two_away = weight_terms(ids, hidden, cot_low, chips, w_proj.shape[0])
    else:
        two_own, two_away = split_terms(
            dot(hidden, cot_low, 0, 0).astype(BF16).reshape(grid + (-1, width)), core
        )
    two_terms = chip_terms(two_own, two_away)
    (full_wproj,) = place(two_pieces, (width,), ids)
    two_terms, cot_low = together(two_terms, cot_low)
    two_plane = scatter_plane(two_terms)
    pre_low, grad_b_fc, grad_ctx, stream_out = feed_back(
        cot_low, hidden, slope, full_wfc, full_wproj, resid + bias_proj
    )
    grad_b_fc = grad_b_fc.reshape(-1)
    grad_ln2_gain = jnp.sum(grad_ctx * normed_two, axis=0)
    grad_ln2_bias = jnp.sum(grad_ctx, axis=0)
    grad_resid = cot_rows + norm_back(grad_ctx * gain_two, normed_two, inv_two)
    grad_b_out = jnp.sum(grad_resid, axis=0)
    resid_low = grad_resid.astype(BF16)
    resid_three = resid_low.reshape(seq_dev, tok_rows, width)
    grad_attn_cols = jnp.einsum(
        "ste,jde->sjdt", resid_three, slot_wout, preferred_element_type=F32
    ).astype(BF16)
    kept = pick(grad_attn_cols, core)
    arrived = to_other_core(pick(grad_attn_cols, 1 - core))
    grad_half = jnp.where(
        core == 0,
        jnp.concatenate([kept, arrived], axis=2),
        jnp.concatenate([arrived, kept], axis=2),
    )
    grad_half, two_plane = together(grad_half, two_plane)
    shard_wproj = scatter_dp(two_plane)
    grad_slots = [grad_half[0]] + [to_xor(grad_half[j], j) for j in range(1, head_count)]

    if aligned:
        one_own, one_away = weight_pair_terms(
            ids, ctx, pre_low, attn_cols, resid_three, chips, own_rows
        )
    else:
        grad_w_fc = dot(ctx, pre_low, 0, 0).astype(BF16)
        grad_w_out = jnp.einsum(
            "sjdt,ste->jde", attn_cols, resid_three, preferred_element_type=F32
        ).astype(BF16)
        grad_w_out = jnp.stack([pick(grad_w_out, head ^ slot) for slot in range(head_count)])
        one_own, one_away = split_terms(
            jnp.concatenate(
                [
                    grad_w_fc.reshape(grid + (-1, hidden_width)),
                    grad_w_out.reshape(grid + (-1, width)),
                ],
                axis=4,
            ),
            core,
        )
    one_terms = chip_terms(one_own, one_away)
    *grad_slots, one_terms = together(*grad_slots, one_terms)
    one_plane = scatter_plane(one_terms)

    _, grad_attn = to_attention(jnp.stack(grad_slots), head)
    grad_attn = grad_attn.reshape(SLOTS, heads, HD, -1)
    grad_qkv = attend_back(me, qkv, attn, grad_attn, lse)
    grad_qkv, shard_wproj = together(grad_qkv, shard_wproj)
    grad_qkv = from_attention(grad_qkv.reshape(SLOTS, 3 * group, -1), head, head_count)

    act_parts = [dot(grad_qkv[slot], group_w, 0, 1) for slot in range(head_count)]
    act_parts = [act_parts[0]] + [part.astype(BF16) for part in act_parts[1:]]
    act_terms = [to_xor(act_parts[j], j) for j in range(1, head_count)]
    grad_group_w = dot(acts[0], grad_qkv[0], 0, 1)
    for slot in range(1, head_count):
        grad_group_w = grad_group_w + dot(acts[slot], grad_qkv[slot], 0, 1)
    token_sums = jnp.sum(grad_qkv.astype(F32), axis=(0, 2)).reshape(3, group)
    grad_bias = jnp.zeros((3, head_count, group), F32)
    grad_bias = lax.dynamic_update_index_in_dim(grad_bias, token_sums, head, 1).reshape(3, width)

    wide_w = group_w.astype(F32)
    act_sum = jnp.sum(wide_w * token_sums.reshape(1, -1), axis=1)
    act_product = jnp.sum(wide_w * grad_group_w, axis=1)
    vectors = [
        act_product,
        act_sum,
        grad_bias[0],
        grad_bias[2],
        grad_b_out,
        grad_ln2_gain,
        grad_ln2_bias,
        grad_b_proj,
        grad_b_fc,
    ]
    packed = jnp.concatenate([v.reshape(devices, -1) for v in vectors], axis=1)
    mine = scatter_small(packed.reshape(grid + (-1,)), core, head, dp)
    grad_group_w = grad_group_w.astype(BF16).reshape(grid + (own_rows, 3 * group))
    half_w = pick(grad_group_w, core, 1).astype(F32) + core_terms(grad_group_w, core).astype(F32)
    shard_w = scatter_z(half_w, dp)
    *near_terms, shard_w, one_plane = together(*act_terms[:2], shard_w, one_plane)
    act_terms = near_terms + act_terms[2:]
    mine, shard_one, shard_wproj, *act_terms = together(
        mine, scatter_dp(one_plane), shard_wproj, *act_terms
    )
    shard_one, shard_wproj = shard_one.astype(F32), shard_wproj.astype(F32)
    sums = plane_total(act_parts[0], act_terms).reshape(2, tok_rows, width)
    grad_act = by_half(
        core, pick(sums, core), to_other_core(pick(sums, 1 - core))
    ).reshape(rows, width)

    pieces = jnp.stack(
        [pick(shard_w, head)]
        + [to_xor(pick(shard_w, head ^ slot), slot) for slot in range(1, head_count)]
    )
    ordered = [pick(pieces, head ^ slot) for slot in range(head_count)]
    shard_wqkv = jnp.concatenate(
        [piece[:, c * group : (c + 1) * group] for c in range(3) for piece in ordered], axis=1
    )

    shard_wfc, shard_wout = shard_one[:, :hidden_width], shard_one[:, hidden_width:]
    grad_rows_in = grad_resid + norm_back(grad_act * gain_one, normed_one, inv_one)

    cut = [mine[edges[i] : edges[i + 1]] for i in range(len(sizes))]
    return (
        stream_out.reshape(seq_dev, tok_rows, width),
        grad_rows_in.reshape(seq_dev, tok_rows, width),
        (cut[0] - ln1_bias.astype(F32) * cut[1]) / ln1_gain.astype(F32),
        cut[1],
        shard_wqkv,
        jnp.stack([cut[2], cut[3]]),
        shard_wout.reshape(-1, width),
        cut[4],
        cut[5],
        cut[6],
        shard_wfc.reshape(-1, hidden_width),
        cut[8],
        shard_wproj.reshape(-1, width),
        cut[7],
    )


def solution(mesh):
    every = ("dp", "blk", "head")
    tokens = P("dp", ("blk", "head"), None)
    vector, matrix = P(every), P(every, None)
    in_specs = (
        tokens,
        vector,
        vector,
        matrix,
        P(None, every),
        matrix,
        vector,
        vector,
        vector,
        matrix,
        vector,
        matrix,
        vector,
        tokens,
    )
    out_specs = (
        tokens,
        tokens,
        vector,
        vector,
        matrix,
        P(None, every),
        matrix,
        vector,
        vector,
        vector,
        matrix,
        vector,
        matrix,
        vector,
    )
    return jax.shard_map(
        on_device, mesh=mesh, in_specs=in_specs, out_specs=out_specs, check_vma=False
    )
```
